32 devices in a mesh: tm: 2 (over x), height: 4 (over z), head: 4 (over y, core).
Axes of the slice: x: 2, y: 2, z: 4, core: 2. Of those that a mesh axis runs over, the one named last changes fastest.
Arguments:
- query_in: bfloat16 [12, 8, 32, 16, 128], P('head', 'tm', 'height'), may hold values from -8 to 8
- key_in: bfloat16 [12, 8, 32, 16, 128], P('head', 'tm', 'height'), may hold values from -8 to 8
- value_in: bfloat16 [12, 8, 32, 16, 128], P('head', 'tm', 'height'), may hold values from -6 to 6
- out_grad: bfloat16 [12, 8, 32, 16, 128], P('head', 'tm', 'height'), may hold values from -6 to 6
Outputs:
- query_grad: bfloat16 [12, 8, 32, 16, 128], P('head', 'tm', 'height')
- key_grad: bfloat16 [12, 8, 32, 16, 128], P('head', 'tm', 'height')
- value_grad: bfloat16 [12, 8, 32, 16, 128], P('head', 'tm', 'height')
The draws below stay inside these ranges and needn't reach their ends.
All inputs are finite; a program needn't handle non-finite values.
Results may differ from the reference program's by a relative error of at most 0.0093.
Values may be sent and summed in bfloat16 or wider, within the bound.
A program may use at most 128 MiB of HBM per device.

```python
import jax
import jax.numpy as jnp
from jax import lax

HEADS = 12
HEAD_DIM = 128
TILE_F = 4
TILE_R = 8
TILE_C = 8
COLS = 16
NF = 8
NR = 32


def draw_pair(key):
    full_shape = (HEADS, NF, NR, COLS, HEAD_DIM)
    seed_list = jax.random.split(jax.random.fold_in(key, 41), 2)
    query_draw = jax.random.truncated_normal(seed_list[0], -4.0, 4.0, full_shape, jnp.float32)
    key_draw = jax.random.truncated_normal(seed_list[1], -4.0, 4.0, full_shape, jnp.float32)
    return (query_draw, key_draw)


def draw_query_in(key, part):
    return draw_pair(key)[0].astype(jnp.bfloat16)


def draw_key_in(key, part):
    return draw_pair(key)[1].astype(jnp.bfloat16)


def levels(rng, shape, pieces, least, high):
    def one(axis_at, blocks):
        draws = jax.random.uniform(jax.random.fold_in(jax.random.fold_in(rng, 6), axis_at), (blocks,), jnp.float32, least / len(pieces), high / len(pieces))
        return jnp.repeat(jnp.exp(draws), shape[axis_at] // blocks).reshape((-1,) + (1,) * (len(shape) - axis_at - 1))

    factor_of = one(*pieces[0])
    for cut in pieces[1:]:
        factor_of = factor_of * one(*cut)
    return factor_of


def centred(own_key, shape, scale, reach, pieces=(), held_as=jnp.bfloat16):
    level = levels(own_key, shape, pieces, -0.22, 0.18) if pieces else 1.0
    array = jax.random.normal(own_key, shape, jnp.float32) * scale * level
    return jnp.minimum(jnp.maximum(array, -reach), reach).astype(held_as)


def setup_inputs(seed: int = 0) -> dict:
    keys = jax.random.split(jax.random.key(seed), 5)
    return {
        "query_in": draw_query_in(jax.random.fold_in(keys[4], 71), 0),
        "key_in": draw_key_in(jax.random.fold_in(keys[4], 71), 0),
        "value_in": centred(keys[2], (HEADS, NF, NR, COLS, HEAD_DIM), 1.0, 6.0, ((0, 4), (1, 2), (2, 4))),
        "out_grad": centred(keys[3], (HEADS, NF, NR, COLS, HEAD_DIM), 1.0, 6.0, ((0, 4), (1, 2), (2, 4))),
    }


def rounded(values):
    return lax.optimization_barrier(values.astype(jnp.bfloat16)).astype(jnp.float32)


def batched(form, left_op, right_op):
    return jnp.einsum(form, left_op.astype(jnp.float32), right_op.astype(jnp.float32))


def corner_at(first, second, third, rank):
    anchor = jnp.zeros((), jnp.int32)
    middle = (first.astype(jnp.int32), second.astype(jnp.int32), third.astype(jnp.int32))
    return (anchor,) + middle + (anchor,) * (rank - 4)


def tiles_back(stacked, grid_f, grid_r, grid_c):
    head_count, tile_f, tile_r, tile_c = stacked.shape[1:5]
    trailing = stacked.shape[5:]
    split = stacked.reshape((grid_f, grid_r, grid_c, head_count, tile_f, tile_r, tile_c) + trailing)
    order = (3, 0, 4, 1, 5, 2, 6) + tuple(range(7, 7 + len(trailing)))
    return split.transpose(order).reshape((head_count, grid_f * tile_f, grid_r * tile_r, grid_c * tile_c) + trailing)


def reference(query_in, key_in, value_in, out_grad):
    head_count, frame_count, row_count, col_count, head_depth = query_in.shape
    score_scale = head_depth ** -0.5
    grid_f = frame_count // TILE_F
    grid_r = row_count // TILE_R
    grid_c = col_count // TILE_C
    border = ((0, 0), (TILE_F, TILE_F), (TILE_R, TILE_R), (TILE_C, TILE_C), (0, 0))
    inside = jnp.pad(jnp.ones((1, frame_count, row_count, col_count, 1), jnp.float32), border)
    tile_shape = (head_count, TILE_F, TILE_R, TILE_C, head_depth)
    span_shape = (head_count, 3 * TILE_F, 3 * TILE_R, 3 * TILE_C, head_depth)
    mask_shape = (1, 3 * TILE_F, 3 * TILE_R, 3 * TILE_C, 1)
    stat_tile = tile_shape[:4]
    stat_span = span_shape[:4]
    key_pad = jnp.pad(key_in, border)
    value_pad = jnp.pad(value_in, border)

    def tile_place(tile_index):
        first = tile_index // (grid_r * grid_c)
        second = (tile_index // grid_c) % grid_r
        third = tile_index % grid_c
        return first * TILE_F, second * TILE_R, third * TILE_C

    def query_tile(tile_index):
        first, second, third = tile_place(tile_index)
        corner = corner_at(first, second, third, 5)
        q_rows = lax.dynamic_slice(query_in, corner, tile_shape).reshape(head_count, -1, head_depth)
        g_rows = lax.dynamic_slice(out_grad, corner, tile_shape).reshape(head_count, -1, head_depth)
        k_span = lax.dynamic_slice(key_pad, corner, span_shape).reshape(head_count, -1, head_depth)
        v_span = lax.dynamic_slice(value_pad, corner, span_shape).reshape(head_count, -1, head_depth)
        live_mask = lax.dynamic_slice(inside, corner, mask_shape).reshape(1, 1, -1) > 0.5
        scores = jnp.where(live_mask, batched("hqd,hkd->hqk", q_rows, k_span) * score_scale, -jnp.inf)
        row_max = jnp.max(scores, axis=-1, keepdims=True)
        log_total = row_max + jnp.log(jnp.sum(jnp.exp(scores - row_max), axis=-1, keepdims=True))
        weights = jnp.exp(scores - log_total)
        weight_bf = rounded(weights)
        attended = batched("hqk,hkd->hqd", weight_bf, v_span)
        row_delta = jnp.sum(g_rows.astype(jnp.float32) * attended, axis=-1, keepdims=True)
        d_weights = batched("hqd,hkd->hqk", g_rows, v_span)
        d_scores = rounded(weights * (d_weights - row_delta))
        grad_rows = batched("hqk,hkd->hqd", d_scores, k_span) * score_scale
        return (grad_rows.astype(jnp.bfloat16).reshape(tile_shape), log_total.reshape(stat_tile), row_delta.reshape(stat_tile))

    tile_ids = jnp.arange(grid_f * grid_r * grid_c, dtype=jnp.int32)
    grad_tiles, total_tiles, delta_tiles = lax.map(query_tile, tile_ids)
    query_grad = tiles_back(grad_tiles, grid_f, grid_r, grid_c)
    log_totals = tiles_back(total_tiles, grid_f, grid_r, grid_c)
    deltas = tiles_back(delta_tiles, grid_f, grid_r, grid_c)
    query_pad = jnp.pad(query_in, border)
    grad_pad = jnp.pad(out_grad, border)
    total_pad = jnp.pad(log_totals, border[:4])
    delta_pad = jnp.pad(deltas, border[:4])

    def key_tile(tile_index):
        first, second, third = tile_place(tile_index)
        corner = corner_at(first, second, third, 5)
        corner_stat = corner_at(first, second, third, 4)
        k_rows = lax.dynamic_slice(key_in, corner, tile_shape).reshape(head_count, -1, head_depth)
        v_rows = lax.dynamic_slice(value_in, corner, tile_shape).reshape(head_count, -1, head_depth)
        q_span = lax.dynamic_slice(query_pad, corner, span_shape).reshape(head_count, -1, head_depth)
        g_span = lax.dynamic_slice(grad_pad, corner, span_shape).reshape(head_count, -1, head_depth)
        total_span = lax.dynamic_slice(total_pad, corner_stat, stat_span).reshape(head_count, -1, 1)
        delta_span = lax.dynamic_slice(delta_pad, corner_stat, stat_span).reshape(head_count, -1, 1)
        live_mask = lax.dynamic_slice(inside, corner, mask_shape).reshape(1, -1, 1) > 0.5
        scores = jnp.where(live_mask, batched("hqd,hkd->hqk", q_span, k_rows) * score_scale, -jnp.inf)
        weights = jnp.exp(scores - total_span)
        weight_bf = rounded(weights)
        d_weights = batched("hqd,hkd->hqk", g_span, v_rows)
        d_scores = rounded(weights * (d_weights - delta_span))
        key_part = batched("hqk,hqd->hkd", d_scores, q_span) * score_scale
        value_part = batched("hqk,hqd->hkd", weight_bf, g_span)
        return (key_part.astype(jnp.bfloat16).reshape(tile_shape), value_part.astype(jnp.bfloat16).reshape(tile_shape))

    key_tiles, value_tiles = lax.map(key_tile, tile_ids)
    key_grad = tiles_back(key_tiles, grid_f, grid_r, grid_c)
    value_grad = tiles_back(value_tiles, grid_f, grid_r, grid_c)
    return query_grad, key_grad, value_grad
```

```python
import functools

import jax
import jax.numpy as jnp
from jax import lax
from jax.experimental import pallas as pl
from jax.experimental.pallas import tpu as pltpu
from jax.sharding import PartitionSpec as P

TILE_C = 8


def shifted(block, axis, distance):
    devices = range(lax.axis_size(axis))
    route = [(i - distance, i) for i in devices if i - distance in devices]
    return lax.ppermute(block, axis, route)


def shortened(x):
    return jax.tree.map(lambda a: a.astype(jnp.bfloat16) if a.dtype == jnp.float32 else a, x)


def extended(x, sides, width):
    for axis, dim in sides:
        size, length = (lax.axis_size(axis), x.shape[dim])
        up = [(i, (i + 1) % size) for i in range(size - 1)]
        down = [(j, i) for i, j in up]
        last = lax.slice_in_dim(x, length - width, length, axis=dim)
        first = lax.slice_in_dim(x, 0, width, axis=dim)
        before = lax.ppermute(last, axis, up)
        after = lax.ppermute(first, axis, down)
        x = jnp.concatenate([before, x, after], axis=dim)
    return x


def neighbour_live():
    offsets = jnp.arange(3, dtype=jnp.int32) - 1
    frame_pos = lax.axis_index("tm") + offsets
    row_pos = lax.axis_index("height") + offsets
    frame_ok = (frame_pos >= 0) & (frame_pos < lax.axis_size("tm"))
    row_ok = (row_pos >= 0) & (row_pos < lax.axis_size("height"))
    return frame_ok[:, None] & row_ok[None, :]


def span_live(neighbour_ok, tile_index, span_start, frame_count, row_count, span_width, col_tile):
    columns = span_start + jnp.arange(span_width, dtype=jnp.int32)
    near_cols = jnp.abs(columns // col_tile - tile_index) <= 1
    live_mask = neighbour_ok[:, :, None, None, None] & near_cols[None, None, None, None, :]
    return jnp.broadcast_to(live_mask, (3, 3, frame_count, row_count, span_width)).reshape(-1)


def scores_of(left_rows, right_rows, live_mask, score_scale):
    raw_scores = (
        jnp.einsum("hqd,hkd->hqk", left_rows, right_rows, preferred_element_type=jnp.float32)
        * score_scale
    )
    return jnp.where(live_mask, raw_scores, -jnp.inf)


def whole_span(array, span_start, span_size, axis_pos):
    return isinstance(span_start, int) and span_start == 0 and (span_size == array.shape[axis_pos])


def cut_span(array, span_start, span_size, axis_pos):
    if whole_span(array, span_start, span_size, axis_pos):
        return array
    return lax.dynamic_slice_in_dim(array, jnp.asarray(span_start, jnp.int32), span_size, axis_pos)


def add_span(array, piece):
    return array + piece


def run_tiles(tile_step, tile_count, col_tile, carried):
    edge_width = 2 * col_tile
    carried = tile_step(0, 0, edge_width, carried)
    return tile_step(tile_count - 1, (tile_count - 2) * col_tile, edge_width, carried)


def send_rows(parts, offset):
    return (
        shifted(parts[0].astype(jnp.bfloat16), "height", offset).astype(jnp.float32),
        shifted(parts[1].astype(jnp.bfloat16), "height", offset).astype(jnp.float32),
    )


def send_frames(parts, offset):
    return shifted((shortened(parts[0]), shortened(parts[1])), "tm", offset)


def local(query_in, key_in, value_in, out_grad):
    head_count, frame_count, row_count, col_count, head_depth = query_in.shape
    col_tile = TILE_C
    tile_count = col_count // col_tile
    score_scale = head_depth ** (-0.5)
    spread_shape = (head_count, 1, 1, frame_count, row_count, col_count, head_depth)
    ext_shape = (head_count, 3, 3, frame_count, row_count, col_count, head_depth)
    stat_shape = (head_count, frame_count, row_count, col_tile)
    neighbour_ok = neighbour_live()
    keys_ext, values_ext = (
        extended(key_in.reshape(spread_shape), (("tm", 1), ("height", 2)), 1),
        extended(value_in.reshape(spread_shape), (("tm", 1), ("height", 2)), 1),
    )

    def query_step(tile_index, span_start, span_width, carried):
        grad_q, row_totals, row_deltas, grad_k, grad_v = carried
        own_start = jnp.asarray(tile_index * col_tile, jnp.int32)
        q_rows = cut_span(query_in, own_start, col_tile, 3).reshape(head_count, -1, head_depth)
        g_rows = cut_span(out_grad, own_start, col_tile, 3).reshape(head_count, -1, head_depth)
        k_span = cut_span(keys_ext, span_start, span_width, 5).reshape(head_count, -1, head_depth)
        v_span = cut_span(values_ext, span_start, span_width, 5).reshape(head_count, -1, head_depth)
        live_mask = span_live(
            neighbour_ok, tile_index, span_start, frame_count, row_count, span_width, col_tile
        )
        scores = scores_of(q_rows, k_span, live_mask[None, None, :], score_scale)
        row_max = jnp.max(scores, axis=-1, keepdims=True)
        log_total = row_max + jnp.log(jnp.sum(jnp.exp(scores - row_max), axis=-1, keepdims=True))
        weights = jnp.exp(scores - log_total)
        weight_bf = weights.astype(jnp.bfloat16)
        attended = jnp.einsum("hqk,hkd->hqd", weight_bf, v_span, preferred_element_type=jnp.float32)
        row_delta = jnp.sum(g_rows.astype(jnp.float32) * attended, axis=-1, keepdims=True)
        d_weights = jnp.einsum("hqd,hkd->hqk", g_rows, v_span, preferred_element_type=jnp.float32)
        d_scores = (weights * (d_weights - row_delta)).astype(jnp.bfloat16)
        grad_piece = (
            jnp.einsum("hqk,hkd->hqd", d_scores, k_span, preferred_element_type=jnp.float32)
            * score_scale
        )
        grad_q = lax.dynamic_update_slice_in_dim(
            grad_q, grad_piece.reshape(stat_shape + (head_depth,)), own_start, 3
        )
        row_totals = lax.dynamic_update_slice_in_dim(
            row_totals, log_total.reshape(stat_shape), own_start, 3
        )
        row_deltas = lax.dynamic_update_slice_in_dim(
            row_deltas, row_delta.reshape(stat_shape), own_start, 3
        )
        span_shape = (head_count, 3, 3, frame_count, row_count, span_width, head_depth)
        key_piece = (
            jnp.einsum("hqk,hqd->hkd", d_scores, q_rows, preferred_element_type=jnp.float32)
            * score_scale
        )
        value_piece = jnp.einsum(
            "hqk,hqd->hkd", weight_bf, g_rows, preferred_element_type=jnp.float32
        )
        grad_k = add_span(grad_k, key_piece.reshape(span_shape))
        grad_v = add_span(grad_v, value_piece.reshape(span_shape))
        return (grad_q, row_totals, row_deltas, grad_k, grad_v)

    stat_full = (head_count, frame_count, row_count, col_count)
    initial = (
        jnp.zeros(query_in.shape, jnp.float32),
        jnp.zeros(stat_full, jnp.float32),
        jnp.zeros(stat_full, jnp.float32),
        jnp.zeros(ext_shape, jnp.float32),
        jnp.zeros(ext_shape, jnp.float32),
    )
    grad_q, row_totals, row_deltas, grad_k, grad_v = run_tiles(
        query_step, tile_count, col_tile, initial
    )
    query_grad = grad_q.astype(jnp.bfloat16)
    from_above = send_rows((grad_k[:, :, 0], grad_v[:, :, 0]), -1)
    from_below = send_rows((grad_k[:, :, 2], grad_v[:, :, 2]), 1)
    part_k = grad_k[:, :, 1] + from_above[0] + from_below[0]
    part_v = grad_v[:, :, 1] + from_above[1] + from_below[1]
    from_next = send_frames((part_k[:, 0], part_v[:, 0]), -1)
    from_prev = send_frames((part_k[:, 2], part_v[:, 2]), 1)
    key_total = part_k[:, 1] + from_next[0] + from_prev[0]
    value_total = part_v[:, 1] + from_next[1] + from_prev[1]
    return (query_grad, key_total.astype(jnp.bfloat16), value_total.astype(jnp.bfloat16))


KEY_STEP = 256
LOG2_E = 1.4426950408889634


def paired_kernel(
    q_in, k_in, v_in, g_in, q_out, k_out, v_out,
    kb, vb, qb, gb, probs, dws, dqt, dk32, dv32, gkb, gvb, got_k, got_v, back,
    loc, xs, xr, zs, zr, gs, gr, bs, br,
):
    head_count, tokens, depth = q_in.shape
    slots = qb.shape[0]
    queries = 2 * tokens
    span = 2 * tokens
    steps = span // KEY_STEP
    scale = depth ** (-0.5)
    x = lax.axis_index("tm")
    z = lax.axis_index("height")
    z_count = lax.axis_size("height")
    parity = lax.rem(x + lax.axis_index("head"), 2)
    other = 1 - x
    inputs = (k_in, v_in, q_in, g_in)

    def head_of(s):
        return 2 * s + parity

    def has(s, par):
        return 2 * s + par < head_count

    def live(d):
        return (z + d - 1 >= 0) & (z + d - 1 < z_count)

    barrier = pltpu.get_barrier_semaphore()
    pl.semaphore_signal(barrier, inc=1, device_id={"tm": other})
    for d in (0, 2):
        @pl.when(live(d))
        def _():
            pl.semaphore_signal(barrier, inc=1, device_id={"height": z + d - 1})
    pl.semaphore_wait(barrier, 1 + jnp.where(live(0), 1, 0) + jnp.where(live(2), 1, 0))

    def room(a, s, f):
        if a == 0:
            return kb.at[s, 1, f]
        if a == 1:
            return vb.at[s, 1, f]
        return (qb if a == 2 else gb).at[s, f]

    def own_copy(a, s):
        return pltpu.make_async_copy(inputs[a].at[head_of(s)], room(a, s, x), loc.at[s, a])

    def swap_send(a, s):
        return pltpu.make_async_remote_copy(
            src_ref=inputs[a].at[2 * s + 1 - parity], dst_ref=room(a, s, x),
            send_sem=xs.at[s, a], recv_sem=xr.at[s, a], device_id={"tm": other},
        )

    def swap_recv(a, s):
        return pltpu.make_async_remote_copy(
            src_ref=inputs[a].at[0], dst_ref=room(a, s, other),
            send_sem=xs.at[s, a], recv_sem=xr.at[s, a], device_id={"tm": other},
        )

    def halo(a, s, d, mine):
        buf = (kb, vb)[a]
        src = inputs[a].at[head_of(s)] if mine else buf.at[s, 1, other]
        part = 0 if mine else 1
        return pltpu.make_async_remote_copy(
            src_ref=src, dst_ref=buf.at[s, 2 - d, x if mine else other],
            send_sem=zs.at[s, d, part, a], recv_sem=zr.at[s, 2 - d, part, a],
            device_id={"height": z + d - 1},
        )

    def halo_recv(a, s, d, mine):
        buf = (kb, vb)[a]
        part = 0 if mine else 1
        return pltpu.make_async_remote_copy(
            src_ref=inputs[a].at[0], dst_ref=buf.at[s, d, x if mine else other],
            send_sem=zs.at[s, d, part, a], recv_sem=zr.at[s, d, part, a],
            device_id={"height": z + d - 1},
        )

    def grad_send(a, s, d):
        return pltpu.make_async_remote_copy(
            src_ref=(gkb, gvb)[a].at[s, d], dst_ref=(got_k, got_v)[a].at[s, 2 - d],
            send_sem=gs.at[s, d, a], recv_sem=gr.at[s, 2 - d, a],
            device_id={"height": z + d - 1},
        )

    def grad_recv(a, s, d):
        return pltpu.make_async_remote_copy(
            src_ref=(gkb, gvb)[a].at[s, d], dst_ref=(got_k, got_v)[a].at[s, d],
            send_sem=gs.at[s, d, a], recv_sem=gr.at[s, d, a],
            device_id={"height": z + d - 1},
        )

    def back_send(a, s):
        return pltpu.make_async_remote_copy(
            src_ref=back.at[s, a], dst_ref=(k_out, v_out, q_out)[a].at[head_of(s)],
            send_sem=bs.at[s, a], recv_sem=br.at[s, a], device_id={"tm": other},
        )

    def back_recv(a, s):
        return pltpu.make_async_remote_copy(
            src_ref=back.at[s, a], dst_ref=(k_out, v_out, q_out)[a].at[2 * s + 1 - parity],
            send_sem=bs.at[s, a], recv_sem=br.at[s, a], device_id={"tm": other},
        )

    for s in range(slots):
        @pl.when(has(s, 1 - parity))
        def _():
            for a in range(4):
                swap_send(a, s).start()

        @pl.when(has(s, parity))
        def _():
            for d in (0, 2):
                @pl.when(live(d))
                def _():
                    for a in range(2):
                        halo(a, s, d, True).start()
            for a in range(4):
                own_copy(a, s).start()

    def forward(s):
        for a in range(2):
            swap_recv(a, s).wait_recv()
            for d in (0, 2):
                @pl.when(live(d))
                def _():
                    halo(a, s, d, False).start()

    def rows_at(d, i):
        return pl.ds(pl.multiple_of(d * span + i * KEY_STEP, KEY_STEP), KEY_STEP)

    def keys_at(ref, s, d, i):
        per = tokens // KEY_STEP
        return ref[s, d, i // per, pl.ds(pl.multiple_of(lax.rem(i, per) * KEY_STEP, KEY_STEP), KEY_STEP), :]

    def folded(block):
        return block.reshape(KEY_STEP // 8, 8, queries)

    def score_pass(s):
        q_rows = qb[s].reshape(queries, depth)

        def over(d, top):
            def one(i, top):
                part = lax.dot_general(
                    keys_at(kb, s, d, i), q_rows, (((1,), (1,)), ((), ())),
                    preferred_element_type=jnp.float32,
                )
                probs[rows_at(d, i), :] = part
                return jnp.maximum(top, jnp.max(folded(part), axis=0))

            return lax.fori_loop(0, jnp.where(live(d), steps, 0), one, top)

        top = over(1, jnp.full((8, queries), -jnp.inf, jnp.float32))
        for d in (0, 2):
            @pl.when(live(d))
            def _():
                for a in range(2):
                    for mine in (True, False):
                        halo_recv(a, s, d, mine).wait_recv()
            top = over(d, top)
        return jnp.max(top, axis=0, keepdims=True)

    def weight_pass(s, top):
        g_rows = gb[s].reshape(queries, depth)

        def one(t, sums):
            d, i = t // steps, lax.rem(t, steps)
            rows = rows_at(d, i)
            prob = jnp.exp2((probs[rows, :] - top) * (scale * LOG2_E))
            dw = lax.dot_general(
                keys_at(vb, s, d, i), g_rows, (((1,), (1,)), ((), ())),
                preferred_element_type=jnp.float32,
            )
            probs[rows, :] = prob
            dws[rows, :] = dw
            return (
                sums[0] + jnp.sum(folded(prob), axis=0),
                sums[1] + jnp.sum(folded(prob * dw), axis=0),
            )

        zero = jnp.zeros((8, queries), jnp.float32)
        first = jnp.where(live(0), 0, steps)
        last = jnp.where(live(2), 3 * steps, 2 * steps)
        total, delta = lax.fori_loop(first, last, one, (zero, zero))
        inverse = 1.0 / jnp.sum(total, axis=0, keepdims=True)
        return inverse, jnp.sum(delta, axis=0, keepdims=True) * inverse

    def grad_pass(s, inverse, delta):
        q_rows = qb[s].reshape(queries, depth)
        g_rows = gb[s].reshape(queries, depth)
        dqt[...] = jnp.zeros_like(dqt)

        @pl.loop(0, 3)
        def _(turn):
            d = lax.rem(turn * 2, 3)

            @pl.when(live(d))
            def _():
                @pl.loop(0, steps)
                def _(i):
                    rows = rows_at(d, i)
                    weight = probs[rows, :] * inverse
                    ds = (weight * (dws[rows, :] - delta)).astype(jnp.bfloat16)
                    dv = jnp.dot(weight.astype(jnp.bfloat16), g_rows, preferred_element_type=jnp.float32)
                    dk = jnp.dot(ds, q_rows, preferred_element_type=jnp.float32) * scale
                    dqt[...] += lax.dot_general(
                        keys_at(kb, s, d, i), ds, (((0,), (0,)), ((), ())),
                        preferred_element_type=jnp.float32,
                    )
                    here = pl.ds(pl.multiple_of(i * KEY_STEP, KEY_STEP), KEY_STEP)
                    gkb[s, d, here, :] = dk.astype(jnp.bfloat16)
                    gvb[s, d, here, :] = dv.astype(jnp.bfloat16)

                    @pl.when(d == 1)
                    def _():
                        dk32[s, here, :] = dk
                        dv32[s, here, :] = dv

                @pl.when(d != 1)
                def _():
                    for a in range(2):
                        grad_send(a, s, d).start()

        dq = (dqt[...].T * scale).astype(jnp.bfloat16).reshape(2, tokens, depth)

        for f in range(2):
            @pl.when(x == f)
            def _():
                q_out[head_of(s)] = dq[f]
                back[s, 2] = dq[1 - f]
        back_send(2, s).start()

    def finish(s):
        for a, full, got, out in ((0, dk32, got_k, k_out), (1, dv32, got_v, v_out)):
            for d in (0, 2):
                @pl.when(live(d))
                def _():
                    grad_recv(a, s, d).wait_recv()
                    full[s] += got[s, d].astype(jnp.float32)
            mine = pl.ds(pl.multiple_of(x * tokens, tokens), tokens)
            theirs = pl.ds(pl.multiple_of(other * tokens, tokens), tokens)
            back[s, a] = full[s, theirs, :].astype(jnp.bfloat16)
            back_send(a, s).start()
            out[head_of(s)] = full[s, mine, :].astype(jnp.bfloat16)

    def ready(s):
        for a in (2, 3):
            swap_recv(a, s).wait_recv()
        for a in range(4):
            own_copy(a, s).wait()

    for s in range(slots):
        if s == 0:
            @pl.when(has(s, parity))
            def _():
                forward(s)
                ready(s)

        @pl.when(has(s, parity))
        def _():
            top = score_pass(s)
            if s + 1 < slots:
                @pl.when(has(s + 1, parity))
                def _():
                    forward(s + 1)
                    ready(s + 1)
            inverse, delta = weight_pass(s, top)
            if s > 0:
                finish(s - 1)
            grad_pass(s, inverse, delta)

            @pl.when(jnp.logical_not(has(s + 1, parity)))
            def _():
                finish(s)

    for s in range(slots):
        @pl.when(has(s, 1 - parity))
        def _():
            for a in range(4):
                swap_send(a, s).wait_send()
            for a in range(3):
                back_recv(a, s).wait_recv()

        @pl.when(has(s, parity))
        def _():
            for d in (0, 2):
                @pl.when(live(d))
                def _():
                    for a in range(2):
                        halo(a, s, d, True).wait_send()
                        halo(a, s, d, False).wait_send()
                        grad_send(a, s, d).wait_send()
            for a in range(3):
                back_send(a, s).wait_send()


def paired(query_in, key_in, value_in, out_grad):
    head_count, frames, rows, cols, depth = query_in.shape
    assert cols == 2 * TILE_C
    tokens = frames * rows * cols
    flat = (head_count, tokens, depth)
    slots = (head_count + 1) // 2
    bf, f32 = jnp.bfloat16, jnp.float32
    dma = pltpu.SemaphoreType.DMA
    outs = pl.pallas_call(
        paired_kernel,
        out_shape=[jax.ShapeDtypeStruct(flat, bf)] * 3,
        in_specs=[pl.BlockSpec(memory_space=pltpu.VMEM)] * 4,
        out_specs=[pl.BlockSpec(memory_space=pltpu.VMEM)] * 3,
        scratch_shapes=[
            pltpu.VMEM((slots, 3, 2, tokens, depth), bf),
            pltpu.VMEM((slots, 3, 2, tokens, depth), bf),
            pltpu.VMEM((slots, 2, tokens, depth), bf),
            pltpu.VMEM((slots, 2, tokens, depth), bf),
            pltpu.VMEM((6 * tokens, 2 * tokens), f32),
            pltpu.VMEM((6 * tokens, 2 * tokens), f32),
            pltpu.VMEM((depth, 2 * tokens), f32),
            pltpu.VMEM((slots, 2 * tokens, depth), f32),
            pltpu.VMEM((slots, 2 * tokens, depth), f32),
            pltpu.VMEM((slots, 3, 2 * tokens, depth), bf),
            pltpu.VMEM((slots, 3, 2 * tokens, depth), bf),
            pltpu.VMEM((slots, 3, 2 * tokens, depth), bf),
            pltpu.VMEM((slots, 3, 2 * tokens, depth), bf),
            pltpu.VMEM((slots, 3, tokens, depth), bf),
            dma((slots, 4)),
            dma((slots, 4)),
            dma((slots, 4)),
            dma((slots, 3, 2, 2)),
            dma((slots, 3, 2, 2)),
            dma((slots, 3, 2)),
            dma((slots, 3, 2)),
            dma((slots, 3)),
            dma((slots, 3)),
        ],
        compiler_params=pltpu.CompilerParams(
            collective_id=0, has_side_effects=True, vmem_limit_bytes=60 * 1024 * 1024
        ),
    )(*(a.reshape(flat) for a in (query_in, key_in, value_in, out_grad)))
    return tuple(o.reshape(query_in.shape) for o in outs)


def solution(mesh):
    return jax.shard_map(
        paired if mesh.shape["tm"] == 2 else local,
        mesh=mesh,
        in_specs=(
            P("head", "tm", "height", None, None),
            P("head", "tm", "height", None, None),
            P("head", "tm", "height", None, None),
            P("head", "tm", "height", None, None),
        ),
        out_specs=(
            P("head", "tm", "height", None, None),
            P("head", "tm", "height", None, None),
            P("head", "tm", "height", None, None),
        ),
        check_vma=False,
    )
```

```python
import jax
import jax.numpy as jnp
from jax import lax
from jax.experimental import pallas as pl
from jax.experimental.pallas import tpu as pltpu
from jax.sharding import PartitionSpec as P

TILE_C = 8


def shifted(block, axis, distance):
    devices = range(lax.axis_size(axis))
    route = [(i - distance, i) for i in devices if i - distance in devices]
    return lax.ppermute(block, axis, route)


def shortened(x):
    return jax.tree.map(lambda a: a.astype(jnp.bfloat16) if a.dtype == jnp.float32 else a, x)


def extended(x, sides, width):
    for axis, dim in sides:
        size, length = (lax.axis_size(axis), x.shape[dim])
        up = [(i, (i + 1) % size) for i in range(size - 1)]
        down = [(j, i) for i, j in up]
        last = lax.slice_in_dim(x, length - width, length, axis=dim)
        first = lax.slice_in_dim(x, 0, width, axis=dim)
        before = lax.ppermute(last, axis, up)
        after = lax.ppermute(first, axis, down)
        x = jnp.concatenate([before, x, after], axis=dim)
    return x


def neighbour_live():
    offsets = jnp.arange(3, dtype=jnp.int32) - 1
    frame_pos = lax.axis_index("tm") + offsets
    row_pos = lax.axis_index("height") + offsets
    frame_ok = (frame_pos >= 0) & (frame_pos < lax.axis_size("tm"))
    row_ok = (row_pos >= 0) & (row_pos < lax.axis_size("height"))
    return frame_ok[:, None] & row_ok[None, :]


def span_live(neighbour_ok, tile_index, span_start, frame_count, row_count, span_width, col_tile):
    columns = span_start + jnp.arange(span_width, dtype=jnp.int32)
    near_cols = jnp.abs(columns // col_tile - tile_index) <= 1
    live_mask = neighbour_ok[:, :, None, None, None] & near_cols[None, None, None, None, :]
    return jnp.broadcast_to(live_mask, (3, 3, frame_count, row_count, span_width)).reshape(-1)


def scores_of(left_rows, right_rows, live_mask, score_scale):
    raw_scores = (
        jnp.einsum("hqd,hkd->hqk", left_rows, right_rows, preferred_element_type=jnp.float32)
        * score_scale
    )
    return jnp.where(live_mask, raw_scores, -jnp.inf)


def whole_span(array, span_start, span_size, axis_pos):
    return isinstance(span_start, int) and span_start == 0 and (span_size == array.shape[axis_pos])


def cut_span(array, span_start, span_size, axis_pos):
    if whole_span(array, span_start, span_size, axis_pos):
        return array
    return lax.dynamic_slice_in_dim(array, jnp.asarray(span_start, jnp.int32), span_size, axis_pos)


def add_span(array, piece):
    return array + piece


def run_tiles(tile_step, tile_count, col_tile, carried):
    edge_width = 2 * col_tile
    carried = tile_step(0, 0, edge_width, carried)
    return tile_step(tile_count - 1, (tile_count - 2) * col_tile, edge_width, carried)


def send_rows(parts, offset):
    return (
        shifted(parts[0].astype(jnp.bfloat16), "height", offset).astype(jnp.float32),
        shifted(parts[1].astype(jnp.bfloat16), "height", offset).astype(jnp.float32),
    )


def send_frames(parts, offset):
    return shifted((shortened(parts[0]), shortened(parts[1])), "tm", offset)


def local(query_in, key_in, value_in, out_grad):
    head_count, frame_count, row_count, col_count, head_depth = query_in.shape
    col_tile = TILE_C
    tile_count = col_count // col_tile
    score_scale = head_depth ** (-0.5)
    spread_shape = (head_count, 1, 1, frame_count, row_count, col_count, head_depth)
    ext_shape = (head_count, 3, 3, frame_count, row_count, col_count, head_depth)
    stat_shape = (head_count, frame_count, row_count, col_tile)
    neighbour_ok = neighbour_live()
    keys_ext, values_ext = (
        extended(key_in.reshape(spread_shape), (("tm", 1), ("height", 2)), 1),
        extended(value_in.reshape(spread_shape), (("tm", 1), ("height", 2)), 1),
    )

    def query_step(tile_index, span_start, span_width, carried):
        grad_q, row_totals, row_deltas, grad_k, grad_v = carried
        own_start = jnp.asarray(tile_index * col_tile, jnp.int32)
        q_rows = cut_span(query_in, own_start, col_tile, 3).reshape(head_count, -1, head_depth)
        g_rows = cut_span(out_grad, own_start, col_tile, 3).reshape(head_count, -1, head_depth)
        k_span = cut_span(keys_ext, span_start, span_width, 5).reshape(head_count, -1, head_depth)
        v_span = cut_span(values_ext, span_start, span_width, 5).reshape(head_count, -1, head_depth)
        live_mask = span_live(
            neighbour_ok, tile_index, span_start, frame_count, row_count, span_width, col_tile
        )
        scores = scores_of(q_rows, k_span, live_mask[None, None, :], score_scale)
        row_max = jnp.max(scores, axis=-1, keepdims=True)
        log_total = row_max + jnp.log(jnp.sum(jnp.exp(scores - row_max), axis=-1, keepdims=True))
        weights = jnp.exp(scores - log_total)
        weight_bf = weights.astype(jnp.bfloat16)
        attended = jnp.einsum("hqk,hkd->hqd", weight_bf, v_span, preferred_element_type=jnp.float32)
        row_delta = jnp.sum(g_rows.astype(jnp.float32) * attended, axis=-1, keepdims=True)
        d_weights = jnp.einsum("hqd,hkd->hqk", g_rows, v_span, preferred_element_type=jnp.float32)
        d_scores = (weights * (d_weights - row_delta)).astype(jnp.bfloat16)
        grad_piece = (
            jnp.einsum("hqk,hkd->hqd", d_scores, k_span, preferred_element_type=jnp.float32)
            * score_scale
        )
        grad_q = lax.dynamic_update_slice_in_dim(
            grad_q, grad_piece.reshape(stat_shape + (head_depth,)), own_start, 3
        )
        row_totals = lax.dynamic_update_slice_in_dim(
            row_totals, log_total.reshape(stat_shape), own_start, 3
        )
        row_deltas = lax.dynamic_update_slice_in_dim(
            row_deltas, row_delta.reshape(stat_shape), own_start, 3
        )
        span_shape = (head_count, 3, 3, frame_count, row_count, span_width, head_depth)
        key_piece = (
            jnp.einsum("hqk,hqd->hkd", d_scores, q_rows, preferred_element_type=jnp.float32)
            * score_scale
        )
        value_piece = jnp.einsum(
            "hqk,hqd->hkd", weight_bf, g_rows, preferred_element_type=jnp.float32
        )
        grad_k = add_span(grad_k, key_piece.reshape(span_shape))
        grad_v = add_span(grad_v, value_piece.reshape(span_shape))
        return (grad_q, row_totals, row_deltas, grad_k, grad_v)

    stat_full = (head_count, frame_count, row_count, col_count)
    initial = (
        jnp.zeros(query_in.shape, jnp.float32),
        jnp.zeros(stat_full, jnp.float32),
        jnp.zeros(stat_full, jnp.float32),
        jnp.zeros(ext_shape, jnp.float32),
        jnp.zeros(ext_shape, jnp.float32),
    )
    grad_q, row_totals, row_deltas, grad_k, grad_v = run_tiles(
        query_step, tile_count, col_tile, initial
    )
    query_grad = grad_q.astype(jnp.bfloat16)
    from_above = send_rows((grad_k[:, :, 0], grad_v[:, :, 0]), -1)
    from_below = send_rows((grad_k[:, :, 2], grad_v[:, :, 2]), 1)
    part_k = grad_k[:, :, 1] + from_above[0] + from_below[0]
    part_v = grad_v[:, :, 1] + from_above[1] + from_below[1]
    from_next = send_frames((part_k[:, 0], part_v[:, 0]), -1)
    from_prev = send_frames((part_k[:, 2], part_v[:, 2]), 1)
    key_total = part_k[:, 1] + from_next[0] + from_prev[0]
    value_total = part_v[:, 1] + from_next[1] + from_prev[1]
    return (query_grad, key_total.astype(jnp.bfloat16), value_total.astype(jnp.bfloat16))


LOG2_E = 1.4426950408889634


def paired_kernel(
    q_in, k_in, v_in, g_in, q_out, k_out, v_out,
    kb, vb, qb, gb, probs, dws, stats, dqt, dk32, dv32, gkb, gvb, got_k, got_v, back,
    loc, xs, xr, zs, zr, gs, gr, bs, br,
):
    head_count, tokens, depth = q_in.shape
    slots = qb.shape[0]
    queries = 2 * tokens
    scale = depth ** (-0.5)
    x = lax.axis_index("tm")
    z = lax.axis_index("height")
    z_count = lax.axis_size("height")
    parity = lax.rem(x + lax.axis_index("head"), 2)
    other = 1 - x
    inputs = (k_in, v_in, q_in, g_in)

    def head_of(s):
        return 2 * s + parity

    def has(s, par):
        return 2 * s + par < head_count

    def live(d):
        return (z + d - 1 >= 0) & (z + d - 1 < z_count)

    barrier = pltpu.get_barrier_semaphore()
    pl.semaphore_signal(barrier, inc=1, device_id={"tm": other})
    for d in (0, 2):
        @pl.when(live(d))
        def _():
            pl.semaphore_signal(barrier, inc=1, device_id={"height": z + d - 1})
    pl.semaphore_wait(barrier, 1 + jnp.where(live(0), 1, 0) + jnp.where(live(2), 1, 0))

    def room(a, s, f):
        if a == 0:
            return kb.at[s, 1, f]
        if a == 1:
            return vb.at[s, 1, f]
        return (qb if a == 2 else gb).at[s, f]

    def own_copy(a, s):
        return pltpu.make_async_copy(inputs[a].at[head_of(s)], room(a, s, x), loc.at[s, a])

    def swap_send(a, s):
        return pltpu.make_async_remote_copy(
            src_ref=inputs[a].at[2 * s + 1 - parity], dst_ref=room(a, s, x),
            send_sem=xs.at[s, a], recv_sem=xr.at[s, a], device_id={"tm": other},
        )

    def swap_recv(a, s):
        return pltpu.make_async_remote_copy(
            src_ref=inputs[a].at[0], dst_ref=room(a, s, other),
            send_sem=xs.at[s, a], recv_sem=xr.at[s, a], device_id={"tm": other},
        )

    def halo(a, s, d, mine):
        buf = (kb, vb)[a]
        src = inputs[a].at[head_of(s)] if mine else buf.at[s, 1, other]
        part = 0 if mine else 1
        return pltpu.make_async_remote_copy(
            src_ref=src, dst_ref=buf.at[s, 2 - d, x if mine else other],
            send_sem=zs.at[s, d, part, a], recv_sem=zr.at[s, 2 - d, part, a],
            device_id={"height": z + d - 1},
        )

    def grad_send(a, s, d, f, part):
        return pltpu.make_async_remote_copy(
            src_ref=(gkb, gvb)[a].at[s, d, f], dst_ref=(got_k, got_v)[a].at[s, 2 - d, f],
            send_sem=gs.at[s, d, part, a], recv_sem=gr.at[s, 2 - d, part, a],
            device_id={"height": z + d - 1},
        )

    def grad_recv(a, s, d, f, part):
        return pltpu.make_async_remote_copy(
            src_ref=(gkb, gvb)[a].at[s, d, f], dst_ref=(got_k, got_v)[a].at[s, d, f],
            send_sem=gs.at[s, d, part, a], recv_sem=gr.at[s, d, part, a],
            device_id={"height": z + d - 1},
        )

    def back_send(a, s):
        return pltpu.make_async_remote_copy(
            src_ref=back.at[s, a], dst_ref=(k_out, v_out, q_out)[a].at[head_of(s)],
            send_sem=bs.at[s, a], recv_sem=br.at[s, a], device_id={"tm": other},
        )

    def back_recv(a, s):
        return pltpu.make_async_remote_copy(
            src_ref=back.at[s, a], dst_ref=(k_out, v_out, q_out)[a].at[2 * s + 1 - parity],
            send_sem=bs.at[s, a], recv_sem=br.at[s, a], device_id={"tm": other},
        )

    def for_live(d, action):
        @pl.when(live(d))
        def _():
            action()

    def send_own_halo(s):
        for a in range(2):
            for d in (0, 2):
                for_live(d, lambda: halo(a, s, d, True).start())

    def forward(s):
        for a in range(2):
            swap_recv(a, s).wait_recv()
            for d in (0, 2):
                for_live(d, lambda: halo(a, s, d, False).start())

    def rows_at(d, f):
        return pl.ds(pl.multiple_of((d * 2 + f) * tokens, tokens), tokens)

    def folded(block):
        return block.reshape(tokens // 8, 8, queries)

    def arrival(turn):
        part = turn // 3
        return lax.rem(1 + 2 * lax.rem(turn, 3), 3), jnp.where(part == 0, x, other), part

    def halo_wait(a, s, d, f, part):
        @pl.when(d != 1)
        def _():
            pltpu.make_async_remote_copy(
                src_ref=inputs[a].at[0], dst_ref=(kb, vb)[a].at[s, d, f],
                send_sem=zs.at[s, d, part, a], recv_sem=zr.at[s, d, part, a],
                device_id={"height": z + d - 1},
            ).wait_recv()

    def score_pass(s, half):
        @pl.loop(3 * half, 3 * half + 3)
        def _(turn):
            d, f, part = arrival(turn)

            @pl.when(live(d))
            def _():
                halo_wait(0, s, d, f, part)
                block = lax.dot_general(
                    kb[s, d, f], qb[s].reshape(queries, depth), (((1,), (1,)), ((), ())),
                    preferred_element_type=jnp.float32,
                )
                probs[rows_at(d, f), :] = block
                stats[0] = jnp.maximum(stats[0], jnp.max(folded(block), axis=0))

    def weight_pass(s):
        stats[1] = jnp.zeros_like(stats[1])
        stats[2] = jnp.zeros_like(stats[2])
        top = jnp.max(stats[0], axis=0, keepdims=True)

        @pl.loop(0, 6)
        def _(turn):
            d, f, part = arrival(turn)

            @pl.when(live(d))
            def _():
                halo_wait(1, s, d, f, part)
                rows = rows_at(d, f)
                prob = jnp.exp2((probs[rows, :] - top) * (scale * LOG2_E))
                dw = lax.dot_general(
                    vb[s, d, f], gb[s].reshape(queries, depth), (((1,), (1,)), ((), ())),
                    preferred_element_type=jnp.float32,
                )
                probs[rows, :] = prob
                dws[rows, :] = dw
                stats[1] += jnp.sum(folded(prob), axis=0)
                stats[2] += jnp.sum(folded(prob * dw), axis=0)

    def grad_pass(s):
        inverse = 1.0 / jnp.sum(stats[1], axis=0, keepdims=True)
        delta = jnp.sum(stats[2], axis=0, keepdims=True) * inverse
        dqt[...] = jnp.zeros_like(dqt)

        @pl.loop(0, 6)
        def _(turn):
            d = lax.rem(2 * lax.rem(turn, 3), 3)
            part = 1 - turn // 3
            f = jnp.where(part == 0, x, other)
            if s > 0:
                @pl.when(turn == 5)
                def _():
                    finish(s - 1)

            @pl.when(live(d))
            def _():
                rows = rows_at(d, f)
                weight = probs[rows, :] * inverse
                ds = (weight * (dws[rows, :] - delta)).astype(jnp.bfloat16)
                dv = jnp.dot(
                    weight.astype(jnp.bfloat16), gb[s].reshape(queries, depth),
                    preferred_element_type=jnp.float32,
                )
                dk = jnp.dot(
                    ds, qb[s].reshape(queries, depth), preferred_element_type=jnp.float32
                ) * scale
                dqt[...] += lax.dot_general(
                    kb[s, d, f], ds, (((0,), (0,)), ((), ())),
                    preferred_element_type=jnp.float32,
                )

                @pl.when(d == 1)
                def _():
                    dk32[s, f] = dk
                    dv32[s, f] = dv

                @pl.when(d != 1)
                def _():
                    gkb[s, d, f] = dk.astype(jnp.bfloat16)
                    gvb[s, d, f] = dv.astype(jnp.bfloat16)
                    for a in range(2):
                        grad_send(a, s, d, f, part).start()

        dq = (dqt[...].T * scale).astype(jnp.bfloat16).reshape(2, tokens, depth)
        for f in range(2):
            @pl.when(x == f)
            def _():
                back[s, 2] = dq[1 - f]
                q_out[head_of(s)] = dq[f]
        back_send(2, s).start()

    def finish(s):
        for part in (1, 0):
            f = other if part else x
            for a, full, got, out in ((0, dk32, got_k, k_out), (1, dv32, got_v, v_out)):
                for d in (0, 2):
                    @pl.when(live(d))
                    def _():
                        grad_recv(a, s, d, f, part).wait_recv()
                        full[s, f] += got[s, d, f].astype(jnp.float32)
                if part:
                    back[s, a] = full[s, f].astype(jnp.bfloat16)
                    back_send(a, s).start()
                else:
                    out[head_of(s)] = full[s, f].astype(jnp.bfloat16)

    for s in range(slots):
        @pl.when(has(s, 1 - parity))
        def _():
            for a in (2, 0, 1, 3):
                swap_send(a, s).start()

        @pl.when(has(s, parity))
        def _():
            if s == 0:
                send_own_halo(s)
            for a in (2, 0, 1, 3):
                own_copy(a, s).start()

    for s in range(slots):
        @pl.when(has(s, parity))
        def _():
            stats[0] = jnp.full_like(stats[0], -jnp.inf)
            for a in (2, 0, 1, 3):
                own_copy(a, s).wait()
            swap_recv(2, s).wait_recv()
            score_pass(s, 0)
            if s == 0:
                forward(s)
                if slots > 1:
                    @pl.when(has(1, parity))
                    def _():
                        send_own_halo(1)
            score_pass(s, 1)
            swap_recv(3, s).wait_recv()
            weight_pass(s)
            if s + 1 < slots:
                @pl.when(has(s + 1, parity))
                def _():
                    if s > 0:
                        send_own_halo(s + 1)
                    forward(s + 1)
            grad_pass(s)

            @pl.when(jnp.logical_not(has(s + 1, parity)))
            def _():
                finish(s)

    for s in range(slots):
        @pl.when(has(s, 1 - parity))
        def _():
            for a in range(4):
                swap_send(a, s).wait_send()
            for a in range(3):
                back_recv(a, s).wait_recv()

        @pl.when(has(s, parity))
        def _():
            for d in (0, 2):
                @pl.when(live(d))
                def _():
                    for a in range(2):
                        for part in range(2):
                            halo(a, s, d, part == 0).wait_send()
                            grad_send(a, s, d, other if part else x, part).wait_send()
            for a in range(3):
                back_send(a, s).wait_send()


def paired(query_in, key_in, value_in, out_grad):
    head_count, frames, rows, cols, depth = query_in.shape
    assert cols == 2 * TILE_C
    tokens = frames * rows * cols
    flat = (head_count, tokens, depth)
    slots = (head_count + 1) // 2
    bf, f32 = jnp.bfloat16, jnp.float32
    dma = pltpu.SemaphoreType.DMA
    outs = pl.pallas_call(
        paired_kernel,
        out_shape=[jax.ShapeDtypeStruct(flat, bf)] * 3,
        in_specs=[pl.BlockSpec(memory_space=pltpu.VMEM)] * 4,
        out_specs=[pl.BlockSpec(memory_space=pltpu.VMEM)] * 3,
        scratch_shapes=[
            pltpu.VMEM((slots, 3, 2, tokens, depth), bf),
            pltpu.VMEM((slots, 3, 2, tokens, depth), bf),
            pltpu.VMEM((slots, 2, tokens, depth), bf),
            pltpu.VMEM((slots, 2, tokens, depth), bf),
            pltpu.VMEM((6 * tokens, 2 * tokens), f32),
            pltpu.VMEM((6 * tokens, 2 * tokens), f32),
            pltpu.VMEM((3, 8, 2 * tokens), f32),
            pltpu.VMEM((depth, 2 * tokens), f32),
            pltpu.VMEM((slots, 2, tokens, depth), f32),
            pltpu.VMEM((slots, 2, tokens, depth), f32),
            pltpu.VMEM((slots, 3, 2, tokens, depth), bf),
            pltpu.VMEM((slots, 3, 2, tokens, depth), bf),
            pltpu.VMEM((slots, 3, 2, tokens, depth), bf),
            pltpu.VMEM((slots, 3, 2, tokens, depth), bf),
            pltpu.VMEM((slots, 3, tokens, depth), bf),
            dma((slots, 4)),
            dma((slots, 4)),
            dma((slots, 4)),
            dma((slots, 3, 2, 2)),
            dma((slots, 3, 2, 2)),
            dma((slots, 3, 2, 2)),
            dma((slots, 3, 2, 2)),
            dma((slots, 3)),
            dma((slots, 3)),
        ],
        compiler_params=pltpu.CompilerParams(
            collective_id=0, has_side_effects=True, vmem_limit_bytes=60 * 1024 * 1024
        ),
    )(*(a.reshape(flat) for a in (query_in, key_in, value_in, out_grad)))
    return tuple(o.reshape(query_in.shape) for o in outs)


def solution(mesh):
    return jax.shard_map(
        paired if mesh.shape["tm"] == 2 else local,
        mesh=mesh,
        in_specs=(
            P("head", "tm", "height", None, None),
            P("head", "tm", "height", None, None),
            P("head", "tm", "height", None, None),
            P("head", "tm", "height", None, None),
        ),
        out_specs=(
            P("head", "tm", "height", None, None),
            P("head", "tm", "height", None, None),
            P("head", "tm", "height", None, None),
        ),
        check_vma=False,
    )
```

```python
import jax
import jax.numpy as jnp
from jax import lax
from jax.experimental import pallas as pl
from jax.experimental.pallas import tpu as pltpu
from jax.sharding import PartitionSpec as P

TILE_C = 8


def shifted(block, axis, distance):
    devices = range(lax.axis_size(axis))
    route = [(i - distance, i) for i in devices if i - distance in devices]
    return lax.ppermute(block, axis, route)


def shortened(x):
    return jax.tree.map(lambda a: a.astype(jnp.bfloat16) if a.dtype == jnp.float32 else a, x)


def extended(x, sides, width):
    for axis, dim in sides:
        size, length = (lax.axis_size(axis), x.shape[dim])
        up = [(i, (i + 1) % size) for i in range(size - 1)]
        down = [(j, i) for i, j in up]
        last = lax.slice_in_dim(x, length - width, length, axis=dim)
        first = lax.slice_in_dim(x, 0, width, axis=dim)
        before = lax.ppermute(last, axis, up)
        after = lax.ppermute(first, axis, down)
        x = jnp.concatenate([before, x, after], axis=dim)
    return x


def neighbour_live():
    offsets = jnp.arange(3, dtype=jnp.int32) - 1
    frame_pos = lax.axis_index("tm") + offsets
    row_pos = lax.axis_index("height") + offsets
    frame_ok = (frame_pos >= 0) & (frame_pos < lax.axis_size("tm"))
    row_ok = (row_pos >= 0) & (row_pos < lax.axis_size("height"))
    return frame_ok[:, None] & row_ok[None, :]


def span_live(neighbour_ok, tile_index, span_start, frame_count, row_count, span_width, col_tile):
    columns = span_start + jnp.arange(span_width, dtype=jnp.int32)
    near_cols = jnp.abs(columns // col_tile - tile_index) <= 1
    live_mask = neighbour_ok[:, :, None, None, None] & near_cols[None, None, None, None, :]
    return jnp.broadcast_to(live_mask, (3, 3, frame_count, row_count, span_width)).reshape(-1)


def scores_of(left_rows, right_rows, live_mask, score_scale):
    raw_scores = (
        jnp.einsum("hqd,hkd->hqk", left_rows, right_rows, preferred_element_type=jnp.float32)
        * score_scale
    )
    return jnp.where(live_mask, raw_scores, -jnp.inf)


def whole_span(array, span_start, span_size, axis_pos):
    return isinstance(span_start, int) and span_start == 0 and (span_size == array.shape[axis_pos])


def cut_span(array, span_start, span_size, axis_pos):
    if whole_span(array, span_start, span_size, axis_pos):
        return array
    return lax.dynamic_slice_in_dim(array, jnp.asarray(span_start, jnp.int32), span_size, axis_pos)


def add_span(array, piece):
    return array + piece


def run_tiles(tile_step, tile_count, col_tile, carried):
    edge_width = 2 * col_tile
    carried = tile_step(0, 0, edge_width, carried)
    return tile_step(tile_count - 1, (tile_count - 2) * col_tile, edge_width, carried)


def send_rows(parts, offset):
    return (
        shifted(parts[0].astype(jnp.bfloat16), "height", offset).astype(jnp.float32),
        shifted(parts[1].astype(jnp.bfloat16), "height", offset).astype(jnp.float32),
    )


def send_frames(parts, offset):
    return shifted((shortened(parts[0]), shortened(parts[1])), "tm", offset)


def local(query_in, key_in, value_in, out_grad):
    head_count, frame_count, row_count, col_count, head_depth = query_in.shape
    col_tile = TILE_C
    tile_count = col_count // col_tile
    score_scale = head_depth ** (-0.5)
    spread_shape = (head_count, 1, 1, frame_count, row_count, col_count, head_depth)
    ext_shape = (head_count, 3, 3, frame_count, row_count, col_count, head_depth)
    stat_shape = (head_count, frame_count, row_count, col_tile)
    neighbour_ok = neighbour_live()
    keys_ext, values_ext = (
        extended(key_in.reshape(spread_shape), (("tm", 1), ("height", 2)), 1),
        extended(value_in.reshape(spread_shape), (("tm", 1), ("height", 2)), 1),
    )

    def query_step(tile_index, span_start, span_width, carried):
        grad_q, row_totals, row_deltas, grad_k, grad_v = carried
        own_start = jnp.asarray(tile_index * col_tile, jnp.int32)
        q_rows = cut_span(query_in, own_start, col_tile, 3).reshape(head_count, -1, head_depth)
        g_rows = cut_span(out_grad, own_start, col_tile, 3).reshape(head_count, -1, head_depth)
        k_span = cut_span(keys_ext, span_start, span_width, 5).reshape(head_count, -1, head_depth)
        v_span = cut_span(values_ext, span_start, span_width, 5).reshape(head_count, -1, head_depth)
        live_mask = span_live(
            neighbour_ok, tile_index, span_start, frame_count, row_count, span_width, col_tile
        )
        scores = scores_of(q_rows, k_span, live_mask[None, None, :], score_scale)
        row_max = jnp.max(scores, axis=-1, keepdims=True)
        log_total = row_max + jnp.log(jnp.sum(jnp.exp(scores - row_max), axis=-1, keepdims=True))
        weights = jnp.exp(scores - log_total)
        weight_bf = weights.astype(jnp.bfloat16)
        attended = jnp.einsum("hqk,hkd->hqd", weight_bf, v_span, preferred_element_type=jnp.float32)
        row_delta = jnp.sum(g_rows.astype(jnp.float32) * attended, axis=-1, keepdims=True)
        d_weights = jnp.einsum("hqd,hkd->hqk", g_rows, v_span, preferred_element_type=jnp.float32)
        d_scores = (weights * (d_weights - row_delta)).astype(jnp.bfloat16)
        grad_piece = (
            jnp.einsum("hqk,hkd->hqd", d_scores, k_span, preferred_element_type=jnp.float32)
            * score_scale
        )
        grad_q = lax.dynamic_update_slice_in_dim(
            grad_q, grad_piece.reshape(stat_shape + (head_depth,)), own_start, 3
        )
        row_totals = lax.dynamic_update_slice_in_dim(
            row_totals, log_total.reshape(stat_shape), own_start, 3
        )
        row_deltas = lax.dynamic_update_slice_in_dim(
            row_deltas, row_delta.reshape(stat_shape), own_start, 3
        )
        span_shape = (head_count, 3, 3, frame_count, row_count, span_width, head_depth)
        key_piece = (
            jnp.einsum("hqk,hqd->hkd", d_scores, q_rows, preferred_element_type=jnp.float32)
            * score_scale
        )
        value_piece = jnp.einsum(
            "hqk,hqd->hkd", weight_bf, g_rows, preferred_element_type=jnp.float32
        )
        grad_k = add_span(grad_k, key_piece.reshape(span_shape))
        grad_v = add_span(grad_v, value_piece.reshape(span_shape))
        return (grad_q, row_totals, row_deltas, grad_k, grad_v)

    stat_full = (head_count, frame_count, row_count, col_count)
    initial = (
        jnp.zeros(query_in.shape, jnp.float32),
        jnp.zeros(stat_full, jnp.float32),
        jnp.zeros(stat_full, jnp.float32),
        jnp.zeros(ext_shape, jnp.float32),
        jnp.zeros(ext_shape, jnp.float32),
    )
    grad_q, row_totals, row_deltas, grad_k, grad_v = run_tiles(
        query_step, tile_count, col_tile, initial
    )
    query_grad = grad_q.astype(jnp.bfloat16)
    from_above = send_rows((grad_k[:, :, 0], grad_v[:, :, 0]), -1)
    from_below = send_rows((grad_k[:, :, 2], grad_v[:, :, 2]), 1)
    part_k = grad_k[:, :, 1] + from_above[0] + from_below[0]
    part_v = grad_v[:, :, 1] + from_above[1] + from_below[1]
    from_next = send_frames((part_k[:, 0], part_v[:, 0]), -1)
    from_prev = send_frames((part_k[:, 2], part_v[:, 2]), 1)
    key_total = part_k[:, 1] + from_next[0] + from_prev[0]
    value_total = part_v[:, 1] + from_next[1] + from_prev[1]
    return (query_grad, key_total.astype(jnp.bfloat16), value_total.astype(jnp.bfloat16))


LOG2_E = 1.4426950408889634


def paired_kernel(
    q_in, k_in, v_in, g_in, q_out, k_out, v_out,
    kb, vb, qb, gb, probs, dws, stats, dqt, dk32, dv32, gkb, gvb, got_k, got_v, back,
    loc, xs, xr, zs, zr, gs, gr, bs, br,
):
    head_count, tokens, depth = q_in.shape
    slots = qb.shape[0]
    queries = 2 * tokens
    scale = depth ** (-0.5)
    x = lax.axis_index("tm")
    z = lax.axis_index("height")
    z_count = lax.axis_size("height")
    parity = lax.rem(x + lax.axis_index("head"), 2)
    other = 1 - x
    inputs = (k_in, v_in, q_in, g_in)

    def head_of(s):
        return 2 * s + parity

    def has(s, par):
        return 2 * s + par < head_count

    def live(d):
        return (z + d - 1 >= 0) & (z + d - 1 < z_count)

    barrier = pltpu.get_barrier_semaphore()
    pl.semaphore_signal(barrier, inc=1, device_id={"tm": other})
    for d in (0, 2):
        @pl.when(live(d))
        def _():
            pl.semaphore_signal(barrier, inc=1, device_id={"height": z + d - 1})
    pl.semaphore_wait(barrier, 1 + jnp.where(live(0), 1, 0) + jnp.where(live(2), 1, 0))

    def room(a, s, f):
        if a == 0:
            return kb.at[s, 1, f]
        if a == 1:
            return vb.at[s, 1, f]
        return (qb if a == 2 else gb).at[s, f]

    def own_copy(a, s):
        return pltpu.make_async_copy(inputs[a].at[head_of(s)], room(a, s, x), loc.at[s, a])

    def swap_send(a, s):
        return pltpu.make_async_remote_copy(
            src_ref=inputs[a].at[2 * s + 1 - parity], dst_ref=room(a, s, x),
            send_sem=xs.at[s, a], recv_sem=xr.at[s, a], device_id={"tm": other},
        )

    def swap_recv(a, s):
        return pltpu.make_async_remote_copy(
            src_ref=inputs[a].at[0], dst_ref=room(a, s, other),
            send_sem=xs.at[s, a], recv_sem=xr.at[s, a], device_id={"tm": other},
        )

    def halo(a, s, d, mine):
        buf = (kb, vb)[a]
        src = inputs[a].at[head_of(s)] if mine else buf.at[s, 1, other]
        part = 0 if mine else 1
        return pltpu.make_async_remote_copy(
            src_ref=src, dst_ref=buf.at[s, 2 - d, x if mine else other],
            send_sem=zs.at[s, d, part, a], recv_sem=zr.at[s, 2 - d, part, a],
            device_id={"height": z + d - 1},
        )

    def grad_send(a, s, d, f, part):
        return pltpu.make_async_remote_copy(
            src_ref=(gkb, gvb)[a].at[s, d, f], dst_ref=(got_k, got_v)[a].at[s, 2 - d, f],
            send_sem=gs.at[s, d, part, a], recv_sem=gr.at[s, 2 - d, part, a],
            device_id={"height": z + d - 1},
        )

    def grad_recv(a, s, d, f, part):
        return pltpu.make_async_remote_copy(
            src_ref=(gkb, gvb)[a].at[s, d, f], dst_ref=(got_k, got_v)[a].at[s, d, f],
            send_sem=gs.at[s, d, part, a], recv_sem=gr.at[s, d, part, a],
            device_id={"height": z + d - 1},
        )

    def back_send(a, s):
        return pltpu.make_async_remote_copy(
            src_ref=back.at[s, a], dst_ref=(k_out, v_out, q_out)[a].at[head_of(s)],
            send_sem=bs.at[s, a], recv_sem=br.at[s, a], device_id={"tm": other},
        )

    def back_recv(a, s):
        return pltpu.make_async_remote_copy(
            src_ref=back.at[s, a], dst_ref=(k_out, v_out, q_out)[a].at[2 * s + 1 - parity],
            send_sem=bs.at[s, a], recv_sem=br.at[s, a], device_id={"tm": other},
        )

    def for_live(d, action):
        @pl.when(live(d))
        def _():
            action()

    def send_own_halo(s):
        for a in range(2):
            for d in (0, 2):
                for_live(d, lambda: halo(a, s, d, True).start())

    def forward(s):
        for a in range(2):
            swap_recv(a, s).wait_recv()
            for d in (0, 2):
                for_live(d, lambda: halo(a, s, d, False).start())

    def rows_at(d, f):
        return pl.ds(pl.multiple_of((d * 2 + f) * tokens, tokens), tokens)

    def folded(block):
        return block.reshape(tokens // 8, 8, queries)

    def arrival(turn):
        part = turn // 3
        return lax.rem(1 + 2 * lax.rem(turn, 3), 3), jnp.where(part == 0, x, other), part

    def halo_wait(a, s, d, f, part):
        @pl.when(d != 1)
        def _():
            pltpu.make_async_remote_copy(
                src_ref=inputs[a].at[0], dst_ref=(kb, vb)[a].at[s, d, f],
                send_sem=zs.at[s, d, part, a], recv_sem=zr.at[s, d, part, a],
                device_id={"height": z + d - 1},
            ).wait_recv()

    def score_pass(s, half):
        @pl.loop(3 * half, 3 * half + 3)
        def _(turn):
            d, f, part = arrival(turn)

            @pl.when(live(d))
            def _():
                halo_wait(0, s, d, f, part)
                block = lax.dot_general(
                    kb[s, d, f], qb[s].reshape(queries, depth), (((1,), (1,)), ((), ())),
                    preferred_element_type=jnp.float32,
                )
                probs[rows_at(d, f), :] = block
                stats[0] = jnp.maximum(stats[0], jnp.max(folded(block), axis=0))

    def weight_pass(s):
        stats[1] = jnp.zeros_like(stats[1])
        stats[2] = jnp.zeros_like(stats[2])
        top = jnp.max(stats[0], axis=0, keepdims=True)

        @pl.loop(0, 6)
        def _(turn):
            d, f, part = arrival(turn)

            @pl.when(live(d))
            def _():
                halo_wait(1, s, d, f, part)
                rows = rows_at(d, f)
                prob = jnp.exp2((probs[rows, :] - top) * (scale * LOG2_E))
                dw = lax.dot_general(
                    vb[s, d, f], gb[s].reshape(queries, depth), (((1,), (1,)), ((), ())),
                    preferred_element_type=jnp.float32,
                )
                probs[rows, :] = prob
                dws[rows, :] = dw
                stats[1] += jnp.sum(folded(prob), axis=0)
                stats[2] += jnp.sum(folded(prob * dw), axis=0)

    def grad_pass(s):
        inverse = 1.0 / jnp.sum(stats[1], axis=0, keepdims=True)
        delta = jnp.sum(stats[2], axis=0, keepdims=True) * inverse
        dqt[...] = jnp.zeros_like(dqt)

        @pl.loop(0, 6)
        def _(turn):
            d = lax.rem(2 * lax.rem(turn, 3), 3)
            part = 1 - turn // 3
            f = jnp.where(part == 0, x, other)
            if s > 0:
                @pl.when(turn == 5)
                def _():
                    finish(s - 1)

            @pl.when(live(d))
            def _():
                rows = rows_at(d, f)
                weight = probs[rows, :] * inverse
                ds = (weight * (dws[rows, :] - delta)).astype(jnp.bfloat16)
                dv = jnp.dot(
                    weight.astype(jnp.bfloat16), gb[s].reshape(queries, depth),
                    preferred_element_type=jnp.float32,
                )
                dk = jnp.dot(
                    ds, qb[s].reshape(queries, depth), preferred_element_type=jnp.float32
                ) * scale
                dqt[...] += lax.dot_general(
                    kb[s, d, f], ds, (((0,), (0,)), ((), ())),
                    preferred_element_type=jnp.float32,
                )

                @pl.when(d == 1)
                def _():
                    dk32[s, f] = dk
                    dv32[s, f] = dv

                @pl.when(d != 1)
                def _():
                    gkb[s, d, f] = dk.astype(jnp.bfloat16)
                    gvb[s, d, f] = dv.astype(jnp.bfloat16)
                    for a in range(2):
                        grad_send(a, s, d, f, part).start()

        dq = (dqt[...].T * scale).astype(jnp.bfloat16).reshape(2, tokens, depth)
        for f in range(2):
            @pl.when(x == f)
            def _():
                back[s, 2] = dq[1 - f]
                q_out[head_of(s)] = dq[f]
        back_send(2, s).start()

    def finish(s):
        for part in (1, 0):
            f = other if part else x
            for a, full, got, out in ((0, dk32, got_k, k_out), (1, dv32, got_v, v_out)):
                for d in (0, 2):
                    @pl.when(live(d))
                    def _():
                        grad_recv(a, s, d, f, part).wait_recv()
                        full[s, f] += got[s, d, f].astype(jnp.float32)
                if part:
                    back[s, a] = full[s, f].astype(jnp.bfloat16)
                    back_send(a, s).start()
                else:
                    out[head_of(s)] = full[s, f].astype(jnp.bfloat16)

    for s in range(slots):
        if s == 0:
            @pl.when(has(s, 1 - parity))
            def _():
                for a in (2, 0, 1, 3):
                    swap_send(a, s).start()

        @pl.when(has(s, parity))
        def _():
            if s == 0:
                send_own_halo(s)
            for a in (2, 0, 1, 3):
                own_copy(a, s).start()

    for s in range(slots):
        @pl.when(has(s, parity))
        def _():
            stats[0] = jnp.full_like(stats[0], -jnp.inf)
            for a in (2, 0, 1, 3):
                own_copy(a, s).wait()
            swap_recv(2, s).wait_recv()
            score_pass(s, 0)
            if s == 0:
                forward(s)
                for t in range(1, slots):
                    @pl.when(has(t, 1 - parity))
                    def _():
                        for a in (2, 0, 1, 3):
                            swap_send(a, t).start()
                if slots > 1:
                    @pl.when(has(1, parity))
                    def _():
                        send_own_halo(1)
            score_pass(s, 1)
            swap_recv(3, s).wait_recv()
            weight_pass(s)
            if s + 1 < slots:
                @pl.when(has(s + 1, parity))
                def _():
                    if s > 0:
                        send_own_halo(s + 1)
                    forward(s + 1)
            grad_pass(s)

            @pl.when(jnp.logical_not(has(s + 1, parity)))
            def _():
                finish(s)

    for s in range(slots):
        @pl.when(has(s, 1 - parity))
        def _():
            for a in range(4):
                swap_send(a, s).wait_send()
            for a in range(3):
                back_recv(a, s).wait_recv()

        @pl.when(has(s, parity))
        def _():
            for d in (0, 2):
                @pl.when(live(d))
                def _():
                    for a in range(2):
                        for part in range(2):
                            halo(a, s, d, part == 0).wait_send()
                            grad_send(a, s, d, other if part else x, part).wait_send()
            for a in range(3):
                back_send(a, s).wait_send()


def settle_kernel(a_in, b_in, c_in, a_out, b_out, c_out, sems):
    pairs = ((a_in, a_out), (b_in, b_out), (c_in, c_out))
    copies = [pltpu.make_async_copy(src, dst, sems.at[i]) for i, (src, dst) in enumerate(pairs)]
    for copy in copies:
        copy.start()
    for copy in copies:
        copy.wait()


def paired(query_in, key_in, value_in, out_grad):
    head_count, frames, rows, cols, depth = query_in.shape
    assert cols == 2 * TILE_C
    tokens = frames * rows * cols
    flat = (head_count, tokens, depth)
    slots = (head_count + 1) // 2
    bf, f32 = jnp.bfloat16, jnp.float32
    dma = pltpu.SemaphoreType.DMA
    outs = pl.pallas_call(
        paired_kernel,
        out_shape=[jax.ShapeDtypeStruct(flat, bf)] * 3,
        in_specs=[pl.BlockSpec(memory_space=pl.ANY)] * 4,
        out_specs=[pl.BlockSpec(memory_space=pltpu.VMEM)] * 3,
        scratch_shapes=[
            pltpu.VMEM((slots, 3, 2, tokens, depth), bf),
            pltpu.VMEM((slots, 3, 2, tokens, depth), bf),
            pltpu.VMEM((slots, 2, tokens, depth), bf),
            pltpu.VMEM((slots, 2, tokens, depth), bf),
            pltpu.VMEM((6 * tokens, 2 * tokens), f32),
            pltpu.VMEM((6 * tokens, 2 * tokens), f32),
            pltpu.VMEM((3, 8, 2 * tokens), f32),
            pltpu.VMEM((depth, 2 * tokens), f32),
            pltpu.VMEM((slots, 2, tokens, depth), f32),
            pltpu.VMEM((slots, 2, tokens, depth), f32),
            pltpu.VMEM((slots, 3, 2, tokens, depth), bf),
            pltpu.VMEM((slots, 3, 2, tokens, depth), bf),
            pltpu.VMEM((slots, 3, 2, tokens, depth), bf),
            pltpu.VMEM((slots, 3, 2, tokens, depth), bf),
            pltpu.VMEM((slots, 3, tokens, depth), bf),
            dma((slots, 4)),
            dma((slots, 4)),
            dma((slots, 4)),
            dma((slots, 3, 2, 2)),
            dma((slots, 3, 2, 2)),
            dma((slots, 3, 2, 2)),
            dma((slots, 3, 2, 2)),
            dma((slots, 3)),
            dma((slots, 3)),
        ],
        compiler_params=pltpu.CompilerParams(
            collective_id=0, has_side_effects=True, vmem_limit_bytes=60 * 1024 * 1024
        ),
    )(*(a.reshape(flat) for a in (query_in, key_in, value_in, out_grad)))
    outs = pl.pallas_call(
        settle_kernel,
        out_shape=[jax.ShapeDtypeStruct(flat, bf)] * 3,
        in_specs=[pl.BlockSpec(memory_space=pltpu.VMEM)] * 3,
        out_specs=[pl.BlockSpec(memory_space=pl.ANY)] * 3,
        scratch_shapes=[dma((3,))],
    )(*outs)
    return tuple(o.reshape(query_in.shape) for o in outs)


def solution(mesh):
    return jax.shard_map(
        paired if mesh.shape["tm"] == 2 else local,
        mesh=mesh,
        in_specs=(
            P("head", "tm", "height", None, None),
            P("head", "tm", "height", None, None),
            P("head", "tm", "height", None, None),
            P("head", "tm", "height", None, None),
        ),
        out_specs=(
            P("head", "tm", "height", None, None),
            P("head", "tm", "height", None, None),
            P("head", "tm", "height", None, None),
        ),
        check_vma=False,
    )
```

```python
import jax
import jax.numpy as jnp
from jax import lax
from jax.experimental import pallas as pl
from jax.experimental.pallas import tpu as pltpu
from jax.sharding import PartitionSpec as P

TILE_C = 8


def shifted(block, axis, distance):
    devices = range(lax.axis_size(axis))
    route = [(i - distance, i) for i in devices if i - distance in devices]
    return lax.ppermute(block, axis, route)


def shortened(x):
    return jax.tree.map(lambda a: a.astype(jnp.bfloat16) if a.dtype == jnp.float32 else a, x)


def extended(x, sides, width):
    for axis, dim in sides:
        size, length = (lax.axis_size(axis), x.shape[dim])
        up = [(i, (i + 1) % size) for i in range(size - 1)]
        down = [(j, i) for i, j in up]
        last = lax.slice_in_dim(x, length - width, length, axis=dim)
        first = lax.slice_in_dim(x, 0, width, axis=dim)
        before = lax.ppermute(last, axis, up)
        after = lax.ppermute(first, axis, down)
        x = jnp.concatenate([before, x, after], axis=dim)
    return x


def neighbour_live():
    offsets = jnp.arange(3, dtype=jnp.int32) - 1
    frame_pos = lax.axis_index("tm") + offsets
    row_pos = lax.axis_index("height") + offsets
    frame_ok = (frame_pos >= 0) & (frame_pos < lax.axis_size("tm"))
    row_ok = (row_pos >= 0) & (row_pos < lax.axis_size("height"))
    return frame_ok[:, None] & row_ok[None, :]


def span_live(neighbour_ok, tile_index, span_start, frame_count, row_count, span_width, col_tile):
    columns = span_start + jnp.arange(span_width, dtype=jnp.int32)
    near_cols = jnp.abs(columns // col_tile - tile_index) <= 1
    live_mask = neighbour_ok[:, :, None, None, None] & near_cols[None, None, None, None, :]
    return jnp.broadcast_to(live_mask, (3, 3, frame_count, row_count, span_width)).reshape(-1)


def scores_of(left_rows, right_rows, live_mask, score_scale):
    raw_scores = (
        jnp.einsum("hqd,hkd->hqk", left_rows, right_rows, preferred_element_type=jnp.float32)
        * score_scale
    )
    return jnp.where(live_mask, raw_scores, -jnp.inf)


def whole_span(array, span_start, span_size, axis_pos):
    return isinstance(span_start, int) and span_start == 0 and (span_size == array.shape[axis_pos])


def cut_span(array, span_start, span_size, axis_pos):
    if whole_span(array, span_start, span_size, axis_pos):
        return array
    return lax.dynamic_slice_in_dim(array, jnp.asarray(span_start, jnp.int32), span_size, axis_pos)


def add_span(array, piece):
    return array + piece


def run_tiles(tile_step, tile_count, col_tile, carried):
    edge_width = 2 * col_tile
    carried = tile_step(0, 0, edge_width, carried)
    return tile_step(tile_count - 1, (tile_count - 2) * col_tile, edge_width, carried)


def send_rows(parts, offset):
    return (
        shifted(parts[0].astype(jnp.bfloat16), "height", offset).astype(jnp.float32),
        shifted(parts[1].astype(jnp.bfloat16), "height", offset).astype(jnp.float32),
    )


def send_frames(parts, offset):
    return shifted((shortened(parts[0]), shortened(parts[1])), "tm", offset)


def local(query_in, key_in, value_in, out_grad):
    head_count, frame_count, row_count, col_count, head_depth = query_in.shape
    col_tile = TILE_C
    tile_count = col_count // col_tile
    score_scale = head_depth ** (-0.5)
    spread_shape = (head_count, 1, 1, frame_count, row_count, col_count, head_depth)
    ext_shape = (head_count, 3, 3, frame_count, row_count, col_count, head_depth)
    stat_shape = (head_count, frame_count, row_count, col_tile)
    neighbour_ok = neighbour_live()
    keys_ext, values_ext = (
        extended(key_in.reshape(spread_shape), (("tm", 1), ("height", 2)), 1),
        extended(value_in.reshape(spread_shape), (("tm", 1), ("height", 2)), 1),
    )

    def query_step(tile_index, span_start, span_width, carried):
        grad_q, row_totals, row_deltas, grad_k, grad_v = carried
        own_start = jnp.asarray(tile_index * col_tile, jnp.int32)
        q_rows = cut_span(query_in, own_start, col_tile, 3).reshape(head_count, -1, head_depth)
        g_rows = cut_span(out_grad, own_start, col_tile, 3).reshape(head_count, -1, head_depth)
        k_span = cut_span(keys_ext, span_start, span_width, 5).reshape(head_count, -1, head_depth)
        v_span = cut_span(values_ext, span_start, span_width, 5).reshape(head_count, -1, head_depth)
        live_mask = span_live(
            neighbour_ok, tile_index, span_start, frame_count, row_count, span_width, col_tile
        )
        scores = scores_of(q_rows, k_span, live_mask[None, None, :], score_scale)
        row_max = jnp.max(scores, axis=-1, keepdims=True)
        log_total = row_max + jnp.log(jnp.sum(jnp.exp(scores - row_max), axis=-1, keepdims=True))
        weights = jnp.exp(scores - log_total)
        weight_bf = weights.astype(jnp.bfloat16)
        attended = jnp.einsum("hqk,hkd->hqd", weight_bf, v_span, preferred_element_type=jnp.float32)
        row_delta = jnp.sum(g_rows.astype(jnp.float32) * attended, axis=-1, keepdims=True)
        d_weights = jnp.einsum("hqd,hkd->hqk", g_rows, v_span, preferred_element_type=jnp.float32)
        d_scores = (weights * (d_weights - row_delta)).astype(jnp.bfloat16)
        grad_piece = (
            jnp.einsum("hqk,hkd->hqd", d_scores, k_span, preferred_element_type=jnp.float32)
            * score_scale
        )
        grad_q = lax.dynamic_update_slice_in_dim(
            grad_q, grad_piece.reshape(stat_shape + (head_depth,)), own_start, 3
        )
        row_totals = lax.dynamic_update_slice_in_dim(
            row_totals, log_total.reshape(stat_shape), own_start, 3
        )
        row_deltas = lax.dynamic_update_slice_in_dim(
            row_deltas, row_delta.reshape(stat_shape), own_start, 3
        )
        span_shape = (head_count, 3, 3, frame_count, row_count, span_width, head_depth)
        key_piece = (
            jnp.einsum("hqk,hqd->hkd", d_scores, q_rows, preferred_element_type=jnp.float32)
            * score_scale
        )
        value_piece = jnp.einsum(
            "hqk,hqd->hkd", weight_bf, g_rows, preferred_element_type=jnp.float32
        )
        grad_k = add_span(grad_k, key_piece.reshape(span_shape))
        grad_v = add_span(grad_v, value_piece.reshape(span_shape))
        return (grad_q, row_totals, row_deltas, grad_k, grad_v)

    stat_full = (head_count, frame_count, row_count, col_count)
    initial = (
        jnp.zeros(query_in.shape, jnp.float32),
        jnp.zeros(stat_full, jnp.float32),
        jnp.zeros(stat_full, jnp.float32),
        jnp.zeros(ext_shape, jnp.float32),
        jnp.zeros(ext_shape, jnp.float32),
    )
    grad_q, row_totals, row_deltas, grad_k, grad_v = run_tiles(
        query_step, tile_count, col_tile, initial
    )
    query_grad = grad_q.astype(jnp.bfloat16)
    from_above = send_rows((grad_k[:, :, 0], grad_v[:, :, 0]), -1)
    from_below = send_rows((grad_k[:, :, 2], grad_v[:, :, 2]), 1)
    part_k = grad_k[:, :, 1] + from_above[0] + from_below[0]
    part_v = grad_v[:, :, 1] + from_above[1] + from_below[1]
    from_next = send_frames((part_k[:, 0], part_v[:, 0]), -1)
    from_prev = send_frames((part_k[:, 2], part_v[:, 2]), 1)
    key_total = part_k[:, 1] + from_next[0] + from_prev[0]
    value_total = part_v[:, 1] + from_next[1] + from_prev[1]
    return (query_grad, key_total.astype(jnp.bfloat16), value_total.astype(jnp.bfloat16))


LOG2_E = 1.4426950408889634


def paired_kernel(
    q_in, k_in, v_in, g_in, q_out, k_out, v_out,
    kb, vb, qb, gb, probs, dws, stats, dqt, dk32, dv32, gkb, gvb, got_k, got_v, back,
    loc, xs, xr, zs, zr, gs, gr, bs, br,
):
    head_count, tokens, depth = q_in.shape
    slots = qb.shape[0]
    queries = 2 * tokens
    scale = depth ** (-0.5)
    x = lax.axis_index("tm")
    z = lax.axis_index("height")
    z_count = lax.axis_size("height")
    parity = lax.rem(x + lax.axis_index("head"), 2)
    other = 1 - x
    inputs = (k_in, v_in, q_in, g_in)

    def head_of(s):
        return 2 * s + parity

    def has(s, par):
        return 2 * s + par < head_count

    def live(d):
        return (z + d - 1 >= 0) & (z + d - 1 < z_count)

    barrier = pltpu.get_barrier_semaphore()
    pl.semaphore_signal(barrier, inc=1, device_id={"tm": other})
    for d in (0, 2):
        @pl.when(live(d))
        def _():
            pl.semaphore_signal(barrier, inc=1, device_id={"height": z + d - 1})
    pl.semaphore_wait(barrier, 1 + jnp.where(live(0), 1, 0) + jnp.where(live(2), 1, 0))

    def room(a, s, f):
        if a == 0:
            return kb.at[s, 1, f]
        if a == 1:
            return vb.at[s, 1, f]
        return (qb if a == 2 else gb).at[s, f]

    def own_copy(a, s):
        return pltpu.make_async_copy(inputs[a].at[head_of(s)], room(a, s, x), loc.at[s, a])

    def swap_send(a, s):
        return pltpu.make_async_remote_copy(
            src_ref=inputs[a].at[2 * s + 1 - parity], dst_ref=room(a, s, x),
            send_sem=xs.at[s, a], recv_sem=xr.at[s, a], device_id={"tm": other},
        )

    def swap_recv(a, s):
        return pltpu.make_async_remote_copy(
            src_ref=inputs[a].at[0], dst_ref=room(a, s, other),
            send_sem=xs.at[s, a], recv_sem=xr.at[s, a], device_id={"tm": other},
        )

    def halo(a, s, d, mine):
        buf = (kb, vb)[a]
        src = inputs[a].at[head_of(s)] if mine else buf.at[s, 1, other]
        part = 0 if mine else 1
        return pltpu.make_async_remote_copy(
            src_ref=src, dst_ref=buf.at[s, 2 - d, x if mine else other],
            send_sem=zs.at[s, d, part, a], recv_sem=zr.at[s, 2 - d, part, a],
            device_id={"height": z + d - 1},
        )

    def grad_send(a, s, d, f, part):
        return pltpu.make_async_remote_copy(
            src_ref=(gkb, gvb)[a].at[s, d, f], dst_ref=(got_k, got_v)[a].at[s, 2 - d, f],
            send_sem=gs.at[s, d, part, a], recv_sem=gr.at[s, 2 - d, part, a],
            device_id={"height": z + d - 1},
        )

    def grad_recv(a, s, d, f, part):
        return pltpu.make_async_remote_copy(
            src_ref=(gkb, gvb)[a].at[s, d, f], dst_ref=(got_k, got_v)[a].at[s, d, f],
            send_sem=gs.at[s, d, part, a], recv_sem=gr.at[s, d, part, a],
            device_id={"height": z + d - 1},
        )

    def back_send(a, s):
        return pltpu.make_async_remote_copy(
            src_ref=back.at[s, a], dst_ref=(k_out, v_out, q_out)[a].at[head_of(s)],
            send_sem=bs.at[s, a], recv_sem=br.at[s, a], device_id={"tm": other},
        )

    def back_recv(a, s):
        return pltpu.make_async_remote_copy(
            src_ref=back.at[s, a], dst_ref=(k_out, v_out, q_out)[a].at[2 * s + 1 - parity],
            send_sem=bs.at[s, a], recv_sem=br.at[s, a], device_id={"tm": other},
        )

    def for_live(d, action):
        @pl.when(live(d))
        def _():
            action()

    def send_own_halo(s):
        for a in range(2):
            for d in (0, 2):
                for_live(d, lambda: halo(a, s, d, True).start())

    def forward(s):
        for a in range(2):
            swap_recv(a, s).wait_recv()
            for d in (0, 2):
                for_live(d, lambda: halo(a, s, d, False).start())

    def rows_at(d, f):
        return pl.ds(pl.multiple_of((d * 2 + f) * tokens, tokens), tokens)

    def folded(block):
        return block.reshape(tokens // 8, 8, queries)

    def arrival(turn):
        part = turn // 3
        return lax.rem(1 + 2 * lax.rem(turn, 3), 3), jnp.where(part == 0, x, other), part

    def halo_wait(a, s, d, f, part):
        @pl.when(d != 1)
        def _():
            pltpu.make_async_remote_copy(
                src_ref=inputs[a].at[0], dst_ref=(kb, vb)[a].at[s, d, f],
                send_sem=zs.at[s, d, part, a], recv_sem=zr.at[s, d, part, a],
                device_id={"height": z + d - 1},
            ).wait_recv()

    def score_pass(s, half):
        @pl.loop(3 * half, 3 * half + 3)
        def _(turn):
            d, f, part = arrival(turn)

            @pl.when(live(d))
            def _():
                halo_wait(0, s, d, f, part)
                block = lax.dot_general(
                    kb[s, d, f], qb[s].reshape(queries, depth), (((1,), (1,)), ((), ())),
                    preferred_element_type=jnp.float32,
                )
                probs[rows_at(d, f), :] = block
                stats[0] = jnp.maximum(stats[0], jnp.max(folded(block), axis=0))

    def weight_pass(s):
        stats[1] = jnp.zeros_like(stats[1])
        stats[2] = jnp.zeros_like(stats[2])
        top = jnp.max(stats[0], axis=0, keepdims=True)

        @pl.loop(0, 6)
        def _(turn):
            d, f, part = arrival(turn)

            @pl.when(live(d))
            def _():
                halo_wait(1, s, d, f, part)
                rows = rows_at(d, f)
                prob = jnp.exp2((probs[rows, :] - top) * (scale * LOG2_E))
                dw = lax.dot_general(
                    vb[s, d, f], gb[s].reshape(queries, depth), (((1,), (1,)), ((), ())),
                    preferred_element_type=jnp.float32,
                )
                probs[rows, :] = prob
                dws[rows, :] = dw
                stats[1] += jnp.sum(folded(prob), axis=0)
                stats[2] += jnp.sum(folded(prob * dw), axis=0)

    def grad_pass(s):
        inverse = 1.0 / jnp.sum(stats[1], axis=0, keepdims=True)
        delta = jnp.sum(stats[2], axis=0, keepdims=True) * inverse
        dqt[...] = jnp.zeros_like(dqt)

        @pl.loop(0, 6)
        def _(turn):
            d = lax.rem(2 * lax.rem(turn, 3), 3)
            part = 1 - turn // 3
            f = jnp.where(part == 0, x, other)
            if s > 0:
                @pl.when(turn == 3)
                def _():
                    finish(s - 1)

            @pl.when(live(d))
            def _():
                rows = rows_at(d, f)
                weight = probs[rows, :] * inverse
                ds = (weight * (dws[rows, :] - delta)).astype(jnp.bfloat16)
                dv = jnp.dot(
                    weight.astype(jnp.bfloat16), gb[s].reshape(queries, depth),
                    preferred_element_type=jnp.float32,
                )
                dk = jnp.dot(
                    ds, qb[s].reshape(queries, depth), preferred_element_type=jnp.float32
                ) * scale
                dqt[...] += lax.dot_general(
                    kb[s, d, f], ds, (((0,), (0,)), ((), ())),
                    preferred_element_type=jnp.float32,
                )

                @pl.when(d == 1)
                def _():
                    dk32[s, f] = dk
                    dv32[s, f] = dv

                @pl.when(d != 1)
                def _():
                    gkb[s, d, f] = dk.astype(jnp.bfloat16)
                    gvb[s, d, f] = dv.astype(jnp.bfloat16)
                    for a in range(2):
                        grad_send(a, s, d, f, part).start()

        dq = (dqt[...].T * scale).astype(jnp.bfloat16).reshape(2, tokens, depth)
        for f in range(2):
            @pl.when(x == f)
            def _():
                back[s, 2] = dq[1 - f]
                q_out[head_of(s)] = dq[f]
        back_send(2, s).start()

    def finish(s):
        for part in (1, 0):
            f = other if part else x
            for a, full, got, out in ((0, dk32, got_k, k_out), (1, dv32, got_v, v_out)):
                for d in (0, 2):
                    @pl.when(live(d))
                    def _():
                        grad_recv(a, s, d, f, part).wait_recv()
                        full[s, f] += got[s, d, f].astype(jnp.float32)
                if part:
                    back[s, a] = full[s, f].astype(jnp.bfloat16)
                    back_send(a, s).start()
                else:
                    out[head_of(s)] = full[s, f].astype(jnp.bfloat16)

    for s in range(slots):
        if s == 0:
            @pl.when(has(s, 1 - parity))
            def _():
                for a in (2, 0, 1, 3):
                    swap_send(a, s).start()

        @pl.when(has(s, parity))
        def _():
            if s == 0:
                send_own_halo(s)
            for a in (2, 0, 1, 3):
                own_copy(a, s).start()

    for s in range(slots):
        @pl.when(has(s, parity))
        def _():
            stats[0] = jnp.full_like(stats[0], -jnp.inf)
            for a in (2, 0, 1, 3):
                own_copy(a, s).wait()
            swap_recv(2, s).wait_recv()
            score_pass(s, 0)
            if s == 0:
                forward(s)
                for t in range(1, slots):
                    @pl.when(has(t, 1 - parity))
                    def _():
                        for a in (2, 0, 1, 3):
                            swap_send(a, t).start()
                if slots > 1:
                    @pl.when(has(1, parity))
                    def _():
                        send_own_halo(1)
            score_pass(s, 1)
            swap_recv(3, s).wait_recv()
            weight_pass(s)
            if s + 1 < slots:
                @pl.when(has(s + 1, parity))
                def _():
                    if s > 0:
                        send_own_halo(s + 1)
                    forward(s + 1)
            grad_pass(s)

            @pl.when(jnp.logical_not(has(s + 1, parity)))
            def _():
                finish(s)

    for s in range(slots):
        @pl.when(has(s, 1 - parity))
        def _():
            for a in range(4):
                swap_send(a, s).wait_send()
            for a in range(3):
                back_recv(a, s).wait_recv()

        @pl.when(has(s, parity))
        def _():
            for d in (0, 2):
                @pl.when(live(d))
                def _():
                    for a in range(2):
                        for part in range(2):
                            halo(a, s, d, part == 0).wait_send()
                            grad_send(a, s, d, other if part else x, part).wait_send()
            for a in range(3):
                back_send(a, s).wait_send()


def settle_kernel(a_in, b_in, c_in, a_out, b_out, c_out, sems):
    pairs = ((a_in, a_out), (b_in, b_out), (c_in, c_out))
    copies = [pltpu.make_async_copy(src, dst, sems.at[i]) for i, (src, dst) in enumerate(pairs)]
    for copy in copies:
        copy.start()
    for copy in copies:
        copy.wait()


def paired(query_in, key_in, value_in, out_grad):
    head_count, frames, rows, cols, depth = query_in.shape
    assert cols == 2 * TILE_C
    tokens = frames * rows * cols
    flat = (head_count, tokens, depth)
    slots = (head_count + 1) // 2
    bf, f32 = jnp.bfloat16, jnp.float32
    dma = pltpu.SemaphoreType.DMA
    outs = pl.pallas_call(
        paired_kernel,
        out_shape=[jax.ShapeDtypeStruct(flat, bf)] * 3,
        in_specs=[pl.BlockSpec(memory_space=pl.ANY)] * 4,
        out_specs=[pl.BlockSpec(memory_space=pltpu.VMEM)] * 3,
        scratch_shapes=[
            pltpu.VMEM((slots, 3, 2, tokens, depth), bf),
            pltpu.VMEM((slots, 3, 2, tokens, depth), bf),
            pltpu.VMEM((slots, 2, tokens, depth), bf),
            pltpu.VMEM((slots, 2, tokens, depth), bf),
            pltpu.VMEM((6 * tokens, 2 * tokens), f32),
            pltpu.VMEM((6 * tokens, 2 * tokens), f32),
            pltpu.VMEM((3, 8, 2 * tokens), f32),
            pltpu.VMEM((depth, 2 * tokens), f32),
            pltpu.VMEM((slots, 2, tokens, depth), f32),
            pltpu.VMEM((slots, 2, tokens, depth), f32),
            pltpu.VMEM((slots, 3, 2, tokens, depth), bf),
            pltpu.VMEM((slots, 3, 2, tokens, depth), bf),
            pltpu.VMEM((slots, 3, 2, tokens, depth), bf),
            pltpu.VMEM((slots, 3, 2, tokens, depth), bf),
            pltpu.VMEM((slots, 3, tokens, depth), bf),
            dma((slots, 4)),
            dma((slots, 4)),
            dma((slots, 4)),
            dma((slots, 3, 2, 2)),
            dma((slots, 3, 2, 2)),
            dma((slots, 3, 2, 2)),
            dma((slots, 3, 2, 2)),
            dma((slots, 3)),
            dma((slots, 3)),
        ],
        compiler_params=pltpu.CompilerParams(
            collective_id=0, has_side_effects=True, vmem_limit_bytes=60 * 1024 * 1024
        ),
    )(*(a.reshape(flat) for a in (query_in, key_in, value_in, out_grad)))
    outs = pl.pallas_call(
        settle_kernel,
        out_shape=[jax.ShapeDtypeStruct(flat, bf)] * 3,
        in_specs=[pl.BlockSpec(memory_space=pltpu.VMEM)] * 3,
        out_specs=[pl.BlockSpec(memory_space=pl.ANY)] * 3,
        scratch_shapes=[dma((3,))],
    )(*outs)
    return tuple(o.reshape(query_in.shape) for o in outs)


def solution(mesh):
    return jax.shard_map(
        paired if mesh.shape["tm"] == 2 else local,
        mesh=mesh,
        in_specs=(
            P("head", "tm", "height", None, None),
            P("head", "tm", "height", None, None),
            P("head", "tm", "height", None, None),
            P("head", "tm", "height", None, None),
        ),
        out_specs=(
            P("head", "tm", "height", None, None),
            P("head", "tm", "height", None, None),
            P("head", "tm", "height", None, None),
        ),
        check_vma=False,
    )
```

```python
import jax
import jax.numpy as jnp
from jax import lax
from jax.experimental import pallas as pl
from jax.experimental.pallas import tpu as pltpu
from jax.sharding import PartitionSpec as P

TILE_C = 8


def shifted(block, axis, distance):
    devices = range(lax.axis_size(axis))
    route = [(i - distance, i) for i in devices if i - distance in devices]
    return lax.ppermute(block, axis, route)


def shortened(x):
    return jax.tree.map(lambda a: a.astype(jnp.bfloat16) if a.dtype == jnp.float32 else a, x)


def extended(x, sides, width):
    for axis, dim in sides:
        size, length = (lax.axis_size(axis), x.shape[dim])
        up = [(i, (i + 1) % size) for i in range(size - 1)]
        down = [(j, i) for i, j in up]
        last = lax.slice_in_dim(x, length - width, length, axis=dim)
        first = lax.slice_in_dim(x, 0, width, axis=dim)
        before = lax.ppermute(last, axis, up)
        after = lax.ppermute(first, axis, down)
        x = jnp.concatenate([before, x, after], axis=dim)
    return x


def neighbour_live():
    offsets = jnp.arange(3, dtype=jnp.int32) - 1
    frame_pos = lax.axis_index("tm") + offsets
    row_pos = lax.axis_index("height") + offsets
    frame_ok = (frame_pos >= 0) & (frame_pos < lax.axis_size("tm"))
    row_ok = (row_pos >= 0) & (row_pos < lax.axis_size("height"))
    return frame_ok[:, None] & row_ok[None, :]


def span_live(neighbour_ok, tile_index, span_start, frame_count, row_count, span_width, col_tile):
    columns = span_start + jnp.arange(span_width, dtype=jnp.int32)
    near_cols = jnp.abs(columns // col_tile - tile_index) <= 1
    live_mask = neighbour_ok[:, :, None, None, None] & near_cols[None, None, None, None, :]
    return jnp.broadcast_to(live_mask, (3, 3, frame_count, row_count, span_width)).reshape(-1)


def scores_of(left_rows, right_rows, live_mask, score_scale):
    raw_scores = (
        jnp.einsum("hqd,hkd->hqk", left_rows, right_rows, preferred_element_type=jnp.float32)
        * score_scale
    )
    return jnp.where(live_mask, raw_scores, -jnp.inf)


def whole_span(array, span_start, span_size, axis_pos):
    return isinstance(span_start, int) and span_start == 0 and (span_size == array.shape[axis_pos])


def cut_span(array, span_start, span_size, axis_pos):
    if whole_span(array, span_start, span_size, axis_pos):
        return array
    return lax.dynamic_slice_in_dim(array, jnp.asarray(span_start, jnp.int32), span_size, axis_pos)


def add_span(array, piece):
    return array + piece


def run_tiles(tile_step, tile_count, col_tile, carried):
    edge_width = 2 * col_tile
    carried = tile_step(0, 0, edge_width, carried)
    return tile_step(tile_count - 1, (tile_count - 2) * col_tile, edge_width, carried)


def send_rows(parts, offset):
    return (
        shifted(parts[0].astype(jnp.bfloat16), "height", offset).astype(jnp.float32),
        shifted(parts[1].astype(jnp.bfloat16), "height", offset).astype(jnp.float32),
    )


def send_frames(parts, offset):
    return shifted((shortened(parts[0]), shortened(parts[1])), "tm", offset)


def local(query_in, key_in, value_in, out_grad):
    head_count, frame_count, row_count, col_count, head_depth = query_in.shape
    col_tile = TILE_C
    tile_count = col_count // col_tile
    score_scale = head_depth ** (-0.5)
    spread_shape = (head_count, 1, 1, frame_count, row_count, col_count, head_depth)
    ext_shape = (head_count, 3, 3, frame_count, row_count, col_count, head_depth)
    stat_shape = (head_count, frame_count, row_count, col_tile)
    neighbour_ok = neighbour_live()
    keys_ext, values_ext = (
        extended(key_in.reshape(spread_shape), (("tm", 1), ("height", 2)), 1),
        extended(value_in.reshape(spread_shape), (("tm", 1), ("height", 2)), 1),
    )

    def query_step(tile_index, span_start, span_width, carried):
        grad_q, row_totals, row_deltas, grad_k, grad_v = carried
        own_start = jnp.asarray(tile_index * col_tile, jnp.int32)
        q_rows = cut_span(query_in, own_start, col_tile, 3).reshape(head_count, -1, head_depth)
        g_rows = cut_span(out_grad, own_start, col_tile, 3).reshape(head_count, -1, head_depth)
        k_span = cut_span(keys_ext, span_start, span_width, 5).reshape(head_count, -1, head_depth)
        v_span = cut_span(values_ext, span_start, span_width, 5).reshape(head_count, -1, head_depth)
        live_mask = span_live(
            neighbour_ok, tile_index, span_start, frame_count, row_count, span_width, col_tile
        )
        scores = scores_of(q_rows, k_span, live_mask[None, None, :], score_scale)
        row_max = jnp.max(scores, axis=-1, keepdims=True)
        log_total = row_max + jnp.log(jnp.sum(jnp.exp(scores - row_max), axis=-1, keepdims=True))
        weights = jnp.exp(scores - log_total)
        weight_bf = weights.astype(jnp.bfloat16)
        attended = jnp.einsum("hqk,hkd->hqd", weight_bf, v_span, preferred_element_type=jnp.float32)
        row_delta = jnp.sum(g_rows.astype(jnp.float32) * attended, axis=-1, keepdims=True)
        d_weights = jnp.einsum("hqd,hkd->hqk", g_rows, v_span, preferred_element_type=jnp.float32)
        d_scores = (weights * (d_weights - row_delta)).astype(jnp.bfloat16)
        grad_piece = (
            jnp.einsum("hqk,hkd->hqd", d_scores, k_span, preferred_element_type=jnp.float32)
            * score_scale
        )
        grad_q = lax.dynamic_update_slice_in_dim(
            grad_q, grad_piece.reshape(stat_shape + (head_depth,)), own_start, 3
        )
        row_totals = lax.dynamic_update_slice_in_dim(
            row_totals, log_total.reshape(stat_shape), own_start, 3
        )
        row_deltas = lax.dynamic_update_slice_in_dim(
            row_deltas, row_delta.reshape(stat_shape), own_start, 3
        )
        span_shape = (head_count, 3, 3, frame_count, row_count, span_width, head_depth)
        key_piece = (
            jnp.einsum("hqk,hqd->hkd", d_scores, q_rows, preferred_element_type=jnp.float32)
            * score_scale
        )
        value_piece = jnp.einsum(
            "hqk,hqd->hkd", weight_bf, g_rows, preferred_element_type=jnp.float32
        )
        grad_k = add_span(grad_k, key_piece.reshape(span_shape))
        grad_v = add_span(grad_v, value_piece.reshape(span_shape))
        return (grad_q, row_totals, row_deltas, grad_k, grad_v)

    stat_full = (head_count, frame_count, row_count, col_count)
    initial = (
        jnp.zeros(query_in.shape, jnp.float32),
        jnp.zeros(stat_full, jnp.float32),
        jnp.zeros(stat_full, jnp.float32),
        jnp.zeros(ext_shape, jnp.float32),
        jnp.zeros(ext_shape, jnp.float32),
    )
    grad_q, row_totals, row_deltas, grad_k, grad_v = run_tiles(
        query_step, tile_count, col_tile, initial
    )
    query_grad = grad_q.astype(jnp.bfloat16)
    from_above = send_rows((grad_k[:, :, 0], grad_v[:, :, 0]), -1)
    from_below = send_rows((grad_k[:, :, 2], grad_v[:, :, 2]), 1)
    part_k = grad_k[:, :, 1] + from_above[0] + from_below[0]
    part_v = grad_v[:, :, 1] + from_above[1] + from_below[1]
    from_next = send_frames((part_k[:, 0], part_v[:, 0]), -1)
    from_prev = send_frames((part_k[:, 2], part_v[:, 2]), 1)
    key_total = part_k[:, 1] + from_next[0] + from_prev[0]
    value_total = part_v[:, 1] + from_next[1] + from_prev[1]
    return (query_grad, key_total.astype(jnp.bfloat16), value_total.astype(jnp.bfloat16))


LOG2_E = 1.4426950408889634


def paired_kernel(
    q_in, k_in, v_in, g_in, q_out, k_out, v_out,
    kb, vb, qb, gb, probs, dws, stats, dqt, dk32, dv32, gkb, gvb, got_k, got_v, back,
    loc, xs, xr, zs, zr, gs, gr, bs, br,
):
    head_count, tokens, depth = q_in.shape
    slots = qb.shape[0]
    queries = 2 * tokens
    scale = depth ** (-0.5)
    x = lax.axis_index("tm")
    z = lax.axis_index("height")
    z_count = lax.axis_size("height")
    parity = lax.rem(x + lax.axis_index("head"), 2)
    other = 1 - x
    inputs = (k_in, v_in, q_in, g_in)

    def head_of(s):
        return 2 * s + parity

    def has(s, par):
        return 2 * s + par < head_count

    def live(d):
        return (z + d - 1 >= 0) & (z + d - 1 < z_count)

    barrier = pltpu.get_barrier_semaphore()
    pl.semaphore_signal(barrier, inc=1, device_id={"tm": other})
    for d in (0, 2):
        @pl.when(live(d))
        def _():
            pl.semaphore_signal(barrier, inc=1, device_id={"height": z + d - 1})
    pl.semaphore_wait(barrier, 1 + jnp.where(live(0), 1, 0) + jnp.where(live(2), 1, 0))

    def room(a, s, f):
        if a == 0:
            return kb.at[s, 1, f]
        if a == 1:
            return vb.at[s, 1, f]
        return (qb if a == 2 else gb).at[s, f]

    def own_copy(a, s):
        return pltpu.make_async_copy(inputs[a].at[head_of(s)], room(a, s, x), loc.at[s, a])

    def swap_send(a, s):
        return pltpu.make_async_remote_copy(
            src_ref=inputs[a].at[2 * s + 1 - parity], dst_ref=room(a, s, x),
            send_sem=xs.at[s, a], recv_sem=xr.at[s, a], device_id={"tm": other},
        )

    def swap_recv(a, s):
        return pltpu.make_async_remote_copy(
            src_ref=inputs[a].at[0], dst_ref=room(a, s, other),
            send_sem=xs.at[s, a], recv_sem=xr.at[s, a], device_id={"tm": other},
        )

    def halo(a, s, d, mine):
        buf = (kb, vb)[a]
        src = inputs[a].at[head_of(s)] if mine else buf.at[s, 1, other]
        part = 0 if mine else 1
        return pltpu.make_async_remote_copy(
            src_ref=src, dst_ref=buf.at[s, 2 - d, x if mine else other],
            send_sem=zs.at[s, d, part, a], recv_sem=zr.at[s, 2 - d, part, a],
            device_id={"height": z + d - 1},
        )

    def grad_send(a, s, d, f, part):
        return pltpu.make_async_remote_copy(
            src_ref=(gkb, gvb)[a].at[s, d, f], dst_ref=(got_k, got_v)[a].at[s, 2 - d, f],
            send_sem=gs.at[s, d, part, a], recv_sem=gr.at[s, 2 - d, part, a],
            device_id={"height": z + d - 1},
        )

    def grad_recv(a, s, d, f, part):
        return pltpu.make_async_remote_copy(
            src_ref=(gkb, gvb)[a].at[s, d, f], dst_ref=(got_k, got_v)[a].at[s, d, f],
            send_sem=gs.at[s, d, part, a], recv_sem=gr.at[s, d, part, a],
            device_id={"height": z + d - 1},
        )

    def back_send(a, s):
        return pltpu.make_async_remote_copy(
            src_ref=back.at[s, a], dst_ref=(k_out, v_out, q_out)[a].at[head_of(s)],
            send_sem=bs.at[s, a], recv_sem=br.at[s, a], device_id={"tm": other},
        )

    def back_recv(a, s):
        return pltpu.make_async_remote_copy(
            src_ref=back.at[s, a], dst_ref=(k_out, v_out, q_out)[a].at[2 * s + 1 - parity],
            send_sem=bs.at[s, a], recv_sem=br.at[s, a], device_id={"tm": other},
        )

    def for_live(d, action):
        @pl.when(live(d))
        def _():
            action()

    def send_own_halo(s):
        for a in range(2):
            for d in (0, 2):
                for_live(d, lambda: halo(a, s, d, True).start())

    def forward(s):
        for a in range(2):
            swap_recv(a, s).wait_recv()
            for d in (0, 2):
                for_live(d, lambda: halo(a, s, d, False).start())

    def rows_at(d, f):
        return pl.ds(pl.multiple_of((d * 2 + f) * tokens, tokens), tokens)

    def folded(block):
        return block.reshape(tokens // 8, 8, queries)

    def arrival(turn):
        part = turn // 3
        return lax.rem(1 + 2 * lax.rem(turn, 3), 3), jnp.where(part == 0, x, other), part

    def halo_wait(a, s, d, f, part):
        @pl.when(d != 1)
        def _():
            pltpu.make_async_remote_copy(
                src_ref=inputs[a].at[0], dst_ref=(kb, vb)[a].at[s, d, f],
                send_sem=zs.at[s, d, part, a], recv_sem=zr.at[s, d, part, a],
                device_id={"height": z + d - 1},
            ).wait_recv()

    def score_pass(s, half):
        @pl.loop(3 * half, 3 * half + 3)
        def _(turn):
            d, f, part = arrival(turn)

            @pl.when(live(d))
            def _():
                halo_wait(0, s, d, f, part)
                block = lax.dot_general(
                    kb[s, d, f], qb[s].reshape(queries, depth), (((1,), (1,)), ((), ())),
                    preferred_element_type=jnp.float32,
                )
                probs[rows_at(d, f), :] = block
                stats[0] = jnp.maximum(stats[0], jnp.max(folded(block), axis=0))

    def weight_pass(s):
        stats[1] = jnp.zeros_like(stats[1])
        stats[2] = jnp.zeros_like(stats[2])
        top = jnp.max(stats[0], axis=0, keepdims=True)

        @pl.loop(0, 6)
        def _(turn):
            d, f, part = arrival(turn)

            @pl.when(live(d))
            def _():
                halo_wait(1, s, d, f, part)
                rows = rows_at(d, f)
                prob = jnp.exp2((probs[rows, :] - top) * (scale * LOG2_E))
                dw = lax.dot_general(
                    vb[s, d, f], gb[s].reshape(queries, depth), (((1,), (1,)), ((), ())),
                    preferred_element_type=jnp.float32,
                )
                probs[rows, :] = prob
                dws[rows, :] = dw
                stats[1] += jnp.sum(folded(prob), axis=0)
                stats[2] += jnp.sum(folded(prob * dw), axis=0)

    def grad_pass(s):
        inverse = 1.0 / jnp.sum(stats[1], axis=0, keepdims=True)
        delta = jnp.sum(stats[2], axis=0, keepdims=True) * inverse
        dqt[...] = jnp.zeros_like(dqt)

        @pl.loop(0, 6)
        def _(turn):
            d = lax.rem(2 * lax.rem(turn, 3), 3)
            part = 1 - turn // 3
            f = jnp.where(part == 0, x, other)
            if s > 0:
                @pl.when(turn == 3)
                def _():
                    finish(s - 1)

            @pl.when(live(d))
            def _():
                rows = rows_at(d, f)
                weight = probs[rows, :] * inverse
                ds = (weight * (dws[rows, :] - delta)).astype(jnp.bfloat16)
                dv = jnp.dot(
                    weight.astype(jnp.bfloat16), gb[s].reshape(queries, depth),
                    preferred_element_type=jnp.float32,
                )
                dk = jnp.dot(
                    ds, qb[s].reshape(queries, depth), preferred_element_type=jnp.float32
                ) * scale
                dqt[...] += lax.dot_general(
                    kb[s, d, f], ds, (((0,), (0,)), ((), ())),
                    preferred_element_type=jnp.float32,
                )

                @pl.when(d == 1)
                def _():
                    dk32[s, f] = dk
                    dv32[s, f] = dv

                @pl.when(d != 1)
                def _():
                    gkb[s, d, f] = dk.astype(jnp.bfloat16)
                    gvb[s, d, f] = dv.astype(jnp.bfloat16)
                    for a in range(2):
                        grad_send(a, s, d, f, part).start()

        dq = (dqt[...].T * scale).astype(jnp.bfloat16).reshape(2, tokens, depth)
        for f in range(2):
            @pl.when(x == f)
            def _():
                back[s, 2] = dq[1 - f]
                q_out[head_of(s)] = dq[f]
        back_send(2, s).start()

    def finish(s):
        for part in (1, 0):
            f = other if part else x
            for a, full, got, out in ((0, dk32, got_k, k_out), (1, dv32, got_v, v_out)):
                for d in (0, 2):
                    @pl.when(live(d))
                    def _():
                        grad_recv(a, s, d, f, part).wait_recv()
                        full[s, f] += got[s, d, f].astype(jnp.float32)
                if part:
                    back[s, a] = full[s, f].astype(jnp.bfloat16)
                    back_send(a, s).start()
                else:
                    out[head_of(s)] = full[s, f].astype(jnp.bfloat16)

    for s in range(slots):
        if s == 0:
            @pl.when(has(s, 1 - parity))
            def _():
                for a in (2, 0, 1, 3):
                    swap_send(a, s).start()

        @pl.when(has(s, parity))
        def _():
            if s == 0:
                send_own_halo(s)
            for a in (2, 0, 1, 3):
                own_copy(a, s).start()

    for s in range(slots):
        @pl.when(has(s, parity))
        def _():
            stats[0] = jnp.full_like(stats[0], -jnp.inf)
            for a in (2, 0, 1, 3):
                own_copy(a, s).wait()
            swap_recv(2, s).wait_recv()
            score_pass(s, 0)
            if s == 0:
                forward(s)
                for t in range(1, slots):
                    @pl.when(has(t, 1 - parity))
                    def _():
                        for a in (2, 0, 1, 3):
                            swap_send(a, t).start()
                if slots > 1:
                    @pl.when(has(1, parity))
                    def _():
                        send_own_halo(1)
            score_pass(s, 1)
            swap_recv(3, s).wait_recv()
            weight_pass(s)
            if s + 1 < slots:
                @pl.when(has(s + 1, parity))
                def _():
                    if s > 0:
                        send_own_halo(s + 1)
                    forward(s + 1)
            grad_pass(s)

            @pl.when(jnp.logical_not(has(s + 1, parity)))
            def _():
                finish(s)

    for s in range(slots):
        @pl.when(has(s, 1 - parity))
        def _():
            for a in range(4):
                swap_send(a, s).wait_send()
            for a in range(3):
                back_recv(a, s).wait_recv()

        @pl.when(has(s, parity))
        def _():
            for d in (0, 2):
                @pl.when(live(d))
                def _():
                    for a in range(2):
                        for part in range(2):
                            halo(a, s, d, part == 0).wait_send()
                            grad_send(a, s, d, other if part else x, part).wait_send()
            for a in range(3):
                back_send(a, s).wait_send()


def settle_kernel(a_in, b_in, c_in, a_out, b_out, c_out, held, sems):
    heads = a_in.shape[0]
    pairs = [(i, h) for h in range(heads) for i in range(3)]
    ins, outs = (a_in, b_in, c_in), (a_out, b_out, c_out)
    loads = [pltpu.make_async_copy(ins[i].at[h], held.at[i, h], sems.at[0, i, h]) for i, h in pairs]
    stores = [pltpu.make_async_copy(held.at[i, h], outs[i].at[h], sems.at[1, i, h]) for i, h in pairs]
    for load in loads:
        load.start()
    for load, store in zip(loads, stores):
        load.wait()
        store.start()
    for store in stores:
        store.wait()


def paired(query_in, key_in, value_in, out_grad):
    head_count, frames, rows, cols, depth = query_in.shape
    assert cols == 2 * TILE_C
    tokens = frames * rows * cols
    flat = (head_count, tokens, depth)
    slots = (head_count + 1) // 2
    bf, f32 = jnp.bfloat16, jnp.float32
    dma = pltpu.SemaphoreType.DMA
    outs = pl.pallas_call(
        paired_kernel,
        out_shape=[jax.ShapeDtypeStruct(flat, bf)] * 3,
        in_specs=[pl.BlockSpec(memory_space=pl.ANY)] * 4,
        out_specs=[pl.BlockSpec(memory_space=pltpu.VMEM)] * 3,
        scratch_shapes=[
            pltpu.VMEM((slots, 3, 2, tokens, depth), bf),
            pltpu.VMEM((slots, 3, 2, tokens, depth), bf),
            pltpu.VMEM((slots, 2, tokens, depth), bf),
            pltpu.VMEM((slots, 2, tokens, depth), bf),
            pltpu.VMEM((6 * tokens, 2 * tokens), f32),
            pltpu.VMEM((6 * tokens, 2 * tokens), f32),
            pltpu.VMEM((3, 8, 2 * tokens), f32),
            pltpu.VMEM((depth, 2 * tokens), f32),
            pltpu.VMEM((slots, 2, tokens, depth), f32),
            pltpu.VMEM((slots, 2, tokens, depth), f32),
            pltpu.VMEM((slots, 3, 2, tokens, depth), bf),
            pltpu.VMEM((slots, 3, 2, tokens, depth), bf),
            pltpu.VMEM((slots, 3, 2, tokens, depth), bf),
            pltpu.VMEM((slots, 3, 2, tokens, depth), bf),
            pltpu.VMEM((slots, 3, tokens, depth), bf),
            dma((slots, 4)),
            dma((slots, 4)),
            dma((slots, 4)),
            dma((slots, 3, 2, 2)),
            dma((slots, 3, 2, 2)),
            dma((slots, 3, 2, 2)),
            dma((slots, 3, 2, 2)),
            dma((slots, 3)),
            dma((slots, 3)),
        ],
        compiler_params=pltpu.CompilerParams(
            collective_id=0, has_side_effects=True, vmem_limit_bytes=60 * 1024 * 1024
        ),
    )(*(a.reshape(flat) for a in (query_in, key_in, value_in, out_grad)))
    outs = pl.pallas_call(
        settle_kernel,
        out_shape=[jax.ShapeDtypeStruct(flat, bf)] * 3,
        in_specs=[pl.BlockSpec(memory_space=pl.ANY)] * 3,
        out_specs=[pl.BlockSpec(memory_space=pl.ANY)] * 3,
        scratch_shapes=[pltpu.VMEM((3, *flat), bf), dma((2, 3, head_count))],
    )(*outs)
    return tuple(o.reshape(query_in.shape) for o in outs)


def solution(mesh):
    return jax.shard_map(
        paired if mesh.shape["tm"] == 2 else local,
        mesh=mesh,
        in_specs=(
            P("head", "tm", "height", None, None),
            P("head", "tm", "height", None, None),
            P("head", "tm", "height", None, None),
            P("head", "tm", "height", None, None),
        ),
        out_specs=(
            P("head", "tm", "height", None, None),
            P("head", "tm", "height", None, None),
            P("head", "tm", "height", None, None),
        ),
        check_vma=False,
    )
```
